32 devices in a mesh: pair: 16 (over z, x, core), cuts: 2 (over y).
Axes of the slice: x: 2, y: 2, z: 4, core: 2. Of those that a mesh axis runs over, the one named last changes fastest.
Arguments:
- amplitudes: bfloat16 [16384, 2048], P('pair'), may hold values from -6 to 6
- factors: bfloat16 [32, 6, 128, 128], P('pair', 'cuts'), may hold values from -0.5 to 0.5
- screening: int32 [8, 16], replicated, may hold values from 0 to 31, as said below
- tile_slot: int32 [32], replicated, may hold values from 0 to 31, as said below
- pair_orbitals: int32 [8, 2], replicated, may hold values from 0 to 3999
- occupied_energy: float32 [4000], replicated, may hold values from -2 to -0.3
- virtual_energy: float32 [32, 128], replicated, may hold values from 0.2 to 3
Outputs:
- scaled_residual: float32 [16384, 2048], P(('pair', 'cuts'))
The draws below stay inside these ranges and needn't reach their ends.
Inputs may be any that keep to these rules, and one draw needn't show every extreme that they name: `screening`: call tile_slot[t] // 2 the owner of tile t. The 16 tiles named by one pair have 16 different owners. `tile_slot`: every tile has its own slot.
All inputs are finite; a program needn't handle non-finite values.
Results may differ from the reference program's by a relative error of at most 0.012.
Values may be sent and summed in bfloat16 or wider, within the bound.
No kernel may reach another device: no remote copies, remote signals or barrier semaphores. Data moves between devices by JAX's collectives and lax.ppermute only.
A program may use at most 64 MiB of HBM per device.

```python
import jax
import jax.numpy as jnp
from jax import lax

TILE = 128
TILE_DEV = 2
K = 16
NQ_CUT = 3
NOCC = 4000
PAIRS = 8
NTILE = 32
NQ = 6
N_CUTS = 2


def shared_layout(key):
    owner_count = NTILE // TILE_DEV
    slot_of_tile = jax.random.permutation(jax.random.fold_in(key, 7), NTILE).astype(jnp.int32)
    tile_of_slot = jnp.argsort(slot_of_tile, stable=True).astype(jnp.int32)
    weights = 2 ** jax.random.randint(jax.random.fold_in(key, 11), (owner_count,), 0, 4)
    raw_scores = jax.random.randint(jax.random.fold_in(key, 13), (PAIRS, owner_count), 0, 65536)
    scores = raw_scores * weights[None, :] * owner_count + jnp.arange(owner_count, dtype=jnp.int32)[None, :]
    top_values, chosen_owners = lax.top_k(scores, K)
    local_index = jax.random.randint(jax.random.fold_in(key, 17), chosen_owners.shape, 0, TILE_DEV)
    slots = chosen_owners.astype(jnp.int32) * TILE_DEV + local_index
    tiles = tile_of_slot[slots]
    return (slot_of_tile, tiles.reshape(PAIRS, K).astype(jnp.int32))


def draw_screening(key, part):
    return shared_layout(key)[1]


def draw_tile_slot(key, part):
    return shared_layout(key)[0]


def plant(array, own_key, low, high):
    spot = [jax.random.randint(jax.random.fold_in(own_key, axis), (), 0, length) for axis, length in enumerate(array.shape)]
    longest = array.shape.index(max(array.shape))
    next_to = spot[:longest] + [(spot[longest] + 1) % array.shape[longest]] + spot[longest + 1:]
    return array.at[tuple(spot)].set(low).at[tuple(next_to)].set(high)


def block_scale(own_key, extent, shards, smallest, high):
    level, own = 1.0, jax.random.fold_in(own_key, 6)
    for position, shards_of in shards:
        draws = jnp.exp(jax.random.uniform(jax.random.fold_in(own, position), (shards_of,), jnp.float32, smallest / len(shards), high / len(shards)))
        level = level * jnp.repeat(draws, extent[position] // shards_of).reshape([-1 if axis == position else 1 for axis in range(len(extent))])
    return level


def noise(stream_key, extent, scale, limit, split=(), kind=jnp.bfloat16):
    values = scale * jax.random.normal(stream_key, extent, jnp.float32)
    if split:
        values = values * block_scale(stream_key, extent, split, -0.22, 0.18)
    return jnp.clip(values, -limit, limit).astype(kind)


def setup_inputs(seed: int = 0) -> dict:
    key_list = jax.random.split(jax.random.key(seed), 8)
    amplitudes = noise(key_list[0], (PAIRS * K * TILE, K * TILE), 1.0, 6.0, ((0, 16),))
    factors = noise(key_list[1], (NTILE, NQ, TILE, TILE), TILE ** -0.5, 0.5, ((0, 16), (1, 2)))
    screening = draw_screening(jax.random.fold_in(key_list[7], 71), 0)
    tile_slot = draw_tile_slot(jax.random.fold_in(key_list[7], 71), 0)
    pair_orbitals = plant(jax.random.randint(key_list[4], (PAIRS, 2), 0, NOCC), jax.random.fold_in(key_list[4], 1), 0, NOCC - 1).astype(jnp.int32)
    occupied_energy = jnp.clip(jax.random.uniform(key_list[5], (NOCC,), jnp.float32, -2.0, -0.3), -2.0, -0.3)
    virtual_energy = jnp.clip(jax.random.uniform(key_list[6], (NTILE, TILE), jnp.float32, 0.2, 3.0), 0.2, 3.0)
    return dict(amplitudes=amplitudes, factors=factors, screening=screening, tile_slot=tile_slot, pair_orbitals=pair_orbitals, occupied_energy=occupied_energy, virtual_energy=virtual_energy)


def reference(amplitudes, factors, screening, tile_slot, pair_orbitals, occupied_energy, virtual_energy):
    def one_pair(inputs):
        block_rows, tiles, orbitals = inputs
        slots = tile_slot[tiles]
        chosen = factors[slots].astype(jnp.float32)
        blocks = block_rows.astype(jnp.float32).reshape(K, TILE, K * TILE)
        ladder = jnp.zeros((K * TILE, K * TILE), jnp.float32)
        for cut_index in range(N_CUTS):
            running = jnp.zeros((K, TILE, K, TILE), jnp.float32)
            for vector in range(NQ_CUT):
                factor_left = chosen[:, cut_index * NQ_CUT + vector]
                half_done = jnp.einsum("iac,icx->iax", factor_left, blocks)
                half_done = lax.optimization_barrier(half_done.astype(jnp.bfloat16)).astype(jnp.float32)
                running = running + jnp.einsum("iajd,jbd->iajb", half_done.reshape(K, TILE, K, TILE), factor_left)
            rounded = lax.optimization_barrier(running.reshape(K * TILE, K * TILE).astype(jnp.bfloat16))
            ladder = ladder + rounded.astype(jnp.float32)
        tile_energy = virtual_energy[tiles].reshape(K * TILE)
        row_energy = tile_energy - occupied_energy[orbitals[0]]
        col_energy = tile_energy - occupied_energy[orbitals[1]]
        return ladder / (row_energy[:, None] + col_energy[None, :])

    stacked = amplitudes.reshape(PAIRS, K * TILE, K * TILE)
    result = lax.map(one_pair, (stacked, screening, pair_orbitals))
    return result.reshape(PAIRS * K * TILE, K * TILE)
```

```python
import functools

import jax
import jax.numpy as jnp
from jax import lax
from jax.experimental import pallas as pl
from jax.experimental.pallas import tpu as pltpu
from jax.sharding import PartitionSpec as P


BOTH = ("pair", "cuts")
ANY = pl.BlockSpec(memory_space=pl.ANY)
SMEM = pl.BlockSpec(memory_space=pltpu.SMEM)
VMEM = pl.BlockSpec(memory_space=pltpu.VMEM)


def pick_kernel(tile_dev, group, screening, tile_slot, factors, *refs):
    outs, sems = refs[:-1], refs[-1]
    count = screening.shape[1]
    me = lax.axis_index("pair")
    copies = []
    for shift, out in enumerate(outs):
        peer = (me // group) ^ shift
        local = jnp.int32(0)
        for t in range(count):
            slot = tile_slot[screening[peer, t]]
            local = jnp.where(slot // tile_dev == me, slot % tile_dev, local)
        copy = pltpu.make_async_copy(factors.at[local], out, sems.at[shift])
        copy.start()
        copies.append(copy)
    for copy in copies:
        copy.wait()


def pick(screening, tile_slot, factors, group, shifts):
    tile_dev, *tail = factors.shape
    return pl.pallas_call(
        functools.partial(pick_kernel, tile_dev, group),
        out_shape=[jax.ShapeDtypeStruct(tail, factors.dtype)] * shifts,
        in_specs=[SMEM, SMEM, VMEM],
        out_specs=[ANY] * shifts,
        scratch_shapes=[pltpu.SemaphoreType.DMA((shifts,))],
        name="pick",
    )(screening, tile_slot, factors)


def ladder_kernel(
    dims, screening, tile_slot, occ, virt, amp, mine, other, out, left, row_den, sem
):
    tile_dev, group, row_tiles, shifts, n_q, tile = dims
    step = pl.program_id(0)
    me, cut = lax.axis_index("pair"), lax.axis_index("cuts")
    pair_id, core = me // group, me % group
    count = screening.shape[1]
    first = core * (count // group) + cut * row_tiles
    half_q = n_q // 2

    @pl.when(step == 0)
    def _():
        for t in range(count):
            slot = tile_slot[screening[pair_id, t]]
            owner = slot // tile_dev
            shift = (owner // group) ^ pair_id
            same = owner % group == core
            for part in range(2):
                dst = left.at[t, pl.ds(part * half_q, half_q)]

                @pl.when(same)
                def _():
                    pltpu.make_async_copy(mine.at[part * shifts + shift], dst, sem).start()

                @pl.when(jnp.logical_not(same))
                def _():
                    pltpu.make_async_copy(other.at[part * shifts + shift], dst, sem).start()

        for i in range(row_tiles):
            row = virt[pl.ds(screening[pair_id, first + i], 1), :] - occ[0]
            row_den[i] = jnp.broadcast_to(row, (tile, tile)).T
        pltpu.make_async_copy(left, left, sem).wait()

    halves = []
    for i in range(row_tiles):
        lhs = left[first + i].reshape(n_q * tile, tile)
        half = jnp.dot(
            lhs, amp[i * tile : (i + 1) * tile, :], preferred_element_type=jnp.float32
        )
        halves.append(half.astype(jnp.bfloat16))
    width = amp.shape[1] // tile
    for j in range(width):
        col = step * width + j
        cols = slice(j * tile, (j + 1) * tile)
        lhs = jnp.concatenate(
            [
                jnp.concatenate([h[q * tile : (q + 1) * tile, cols] for q in range(n_q)], axis=1)
                for h in halves
            ],
            axis=0,
        )
        rhs = jnp.concatenate([left[col, q] for q in range(n_q)], axis=1)
        acc = lax.dot_general(
            lhs, rhs, (((1,), (1,)), ((), ())), preferred_element_type=jnp.float32
        )
        col_e = virt[pl.ds(screening[pair_id, col], 1), :] - occ[1]
        for i in range(row_tiles):
            rows = slice(i * tile, (i + 1) * tile)
            out[rows, cols] = acc[rows] / (row_den[i] + col_e)


def ladder(screening, tile_slot, occ, virt, amplitudes, mine, other, dims, cut):
    tile_dev, group, row_tiles, shifts, n_q, tile = dims
    columns = amplitudes.shape[1]
    rows, wide = row_tiles * tile, 2 * tile
    return pl.pallas_call(
        functools.partial(ladder_kernel, dims),
        out_shape=jax.ShapeDtypeStruct((rows, columns), jnp.float32),
        grid=(columns // wide,),
        in_specs=[
            SMEM,
            SMEM,
            SMEM,
            VMEM,
            pl.BlockSpec((rows, wide), lambda c: (lax.axis_index("cuts"), c)),
            ANY,
            ANY,
        ],
        out_specs=pl.BlockSpec((rows, wide), lambda c: (0, c)),
        scratch_shapes=[
            pltpu.VMEM((screening.shape[1], n_q, tile, tile), jnp.bfloat16),
            pltpu.VMEM((row_tiles, tile, tile), jnp.float32),
            pltpu.SemaphoreType.DMA,
        ],
        name="ladder",
    )(screening, tile_slot, occ, virt, amplitudes, mine, other)


def direct(
    amplitudes, factors, screening, tile_slot, pair_orbitals, occupied_energy, virtual_energy
):
    tile_dev, q_cut, tile, _ = factors.shape
    n_pair, n_cut = lax.axis_size("pair"), lax.axis_size("cuts")
    group = n_pair // screening.shape[0]
    shifts = n_pair // group
    row_tiles = amplitudes.shape[0] // tile // n_cut
    me = lax.axis_index("pair")

    def send(x, move):
        pairs = [
            (p * n_cut + c, dst[0] * n_cut + dst[1])
            for p in range(n_pair)
            for c in range(n_cut)
            for dst in [move(p, c)]
        ]
        return lax.ppermute(x, BOTH, pairs)

    picked = pick(screening, tile_slot, factors, group, shifts)
    got = [picked[0]] + [
        send(picked[s], lambda p, c: (p ^ (s * group), c)) for s in range(1, shifts)
    ]
    crossed = [send(x, lambda p, c: (p, c ^ 1)) for x in got]
    mine = jnp.stack(got + crossed)
    other = send(mine, lambda p, c: (p ^ 1, c))
    occ = occupied_energy[pair_orbitals[me // group]]
    dims = (tile_dev, group, row_tiles, shifts, q_cut * n_cut, tile)
    return ladder(
        screening, tile_slot, occ, virtual_energy, amplitudes, mine, other, dims, None
    )


def general(
    amplitudes, factors, screening, tile_slot, pair_orbitals, occupied_energy, virtual_energy
):
    tile_dev, q_cut, tile, _ = factors.shape
    count = screening.shape[1]
    me = lax.axis_index("pair")
    row_tiles = amplitudes.shape[0] // tile
    first_tile = me * row_tiles
    pair_id, tile_start = first_tile // count, first_tile % count
    my_tiles = screening[pair_id]
    my_slots = tile_slot[my_tiles]
    device_pairs = jnp.arange(lax.axis_size("pair"), dtype=jnp.int32) * row_tiles // count
    slot_table = tile_slot[screening[device_pairs]]
    wanted = slot_table // tile_dev == me
    local = jnp.sum(jnp.where(wanted, slot_table % tile_dev, 0), axis=1)
    needed = jnp.any(wanted, axis=1)
    outgoing = jnp.where(
        needed[:, None, None, None], factors[local], jnp.zeros((), factors.dtype)
    )
    incoming = lax.all_to_all(outgoing, "pair", split_axis=0, concat_axis=0, tiled=True)
    chosen = incoming[my_slots // tile_dev]
    left = lax.dynamic_slice_in_dim(chosen, tile_start, row_tiles, 0)
    blocks = amplitudes.reshape(row_tiles, tile, count * tile)
    total = jnp.zeros((row_tiles, tile, count, tile), jnp.float32)
    for q in range(q_cut):
        half = jnp.einsum(
            "iac,icx->iax", left[:, q], blocks, preferred_element_type=jnp.float32
        )
        half = half.astype(jnp.bfloat16).reshape(row_tiles, tile, count, tile)
        total = total + jnp.einsum(
            "iajd,jbd->iajb", half, chosen[:, q], preferred_element_type=jnp.float32
        )
    partial = total.reshape(row_tiles * tile, count * tile).astype(jnp.bfloat16)
    summed = lax.psum_scatter(partial, "cuts", scatter_dimension=0, tiled=True)
    occ = occupied_energy[pair_orbitals[pair_id]]
    energy = virtual_energy[my_tiles].reshape(count * tile)
    rows = summed.shape[0]
    begin = tile_start * tile + lax.axis_index("cuts") * rows
    row_energy = lax.dynamic_slice_in_dim(energy - occ[0], begin, rows, 0)
    return summed.astype(jnp.float32) / (row_energy[:, None] + (energy - occ[1])[None, :])


def solution(mesh):
    n_pair, n_cut = mesh.shape["pair"], mesh.shape["cuts"]

    def local(amplitudes, factors, screening, *rest):
        n_pos, count = screening.shape
        every_owner = count == n_pair and n_pair == 2 * n_pos and n_pos & (n_pos - 1) == 0
        body = direct if every_owner and n_cut == 2 else general
        return body(amplitudes, factors, screening, *rest)

    return jax.shard_map(
        local,
        mesh=mesh,
        in_specs=(P("pair", None), P("pair", "cuts", None, None), P(), P(), P(), P(), P()),
        out_specs=P(BOTH, None),
        check_vma=False,
    )
```

```python
import functools

import jax
import jax.numpy as jnp
from jax import lax
from jax.experimental import pallas as pl
from jax.experimental.pallas import tpu as pltpu
from jax.sharding import PartitionSpec as P


BOTH = ("pair", "cuts")
ANY = pl.BlockSpec(memory_space=pl.ANY)
SMEM = pl.BlockSpec(memory_space=pltpu.SMEM)
VMEM = pl.BlockSpec(memory_space=pltpu.VMEM)


def pick_kernel(tile_dev, group, screening, tile_slot, factors, *refs):
    outs, sems = refs[:-1], refs[-1]
    count = screening.shape[1]
    me = lax.axis_index("pair")
    copies = []
    for shift, out in enumerate(outs):
        peer = (me // group) ^ shift
        local = jnp.int32(0)
        for t in range(count):
            slot = tile_slot[screening[peer, t]]
            local = jnp.where(slot // tile_dev == me, slot % tile_dev, local)
        copy = pltpu.make_async_copy(factors.at[local], out, sems.at[shift])
        copy.start()
        copies.append(copy)
    for copy in copies:
        copy.wait()


def pick(screening, tile_slot, factors, group, shifts):
    tile_dev, *tail = factors.shape
    return pl.pallas_call(
        functools.partial(pick_kernel, tile_dev, group),
        out_shape=[jax.ShapeDtypeStruct(tail, factors.dtype)] * shifts,
        in_specs=[SMEM, SMEM, VMEM],
        out_specs=[ANY] * shifts,
        scratch_shapes=[pltpu.SemaphoreType.DMA((shifts,))],
        name="pick",
    )(screening, tile_slot, factors)


def ladder_kernel(
    dims, screening, tile_slot, occ, virt, amp, *refs
):
    tile_dev, group, row_tiles, shifts, n_q, tile, wide = dims
    mine, other, (out, left, row_den, held, sem, out_sem) = refs[:3], refs[3:6], refs[6:]
    me, cut = lax.axis_index("pair"), lax.axis_index("cuts")
    pair_id, core = me // group, me % group
    count = screening.shape[1]
    first = core * (count // group) + cut * row_tiles
    half_q, half_s = n_q // 2, shifts // 2

    for t in range(count):
        slot = tile_slot[screening[pair_id, t]]
        owner = slot // tile_dev
        shift = (owner // group) ^ pair_id
        same = owner % group == core
        near = shift < half_s
        far = shift - half_s
        for part in range(2):
            dst = left.at[t, pl.ds(part * half_q, half_q)]
            for held_by, bufs in ((same, mine), (jnp.logical_not(same), other)):

                @pl.when(held_by & near)
                def _():
                    pltpu.make_async_copy(bufs[0].at[part * half_s + shift], dst, sem).start()

                @pl.when(held_by & jnp.logical_not(near))
                def _():
                    pltpu.make_async_copy(bufs[1 + part].at[far], dst, sem).start()

    for i in range(row_tiles):
        row = virt[pl.ds(screening[pair_id, first + i], 1), :] - occ[0]
        row_den[i] = jnp.broadcast_to(row, (tile, tile)).T
    pltpu.make_async_copy(left, left, sem).wait()

    def write(step, slot):
        at = pl.ds(pl.multiple_of(step * wide, wide), wide)
        return pltpu.make_async_copy(held.at[slot], out.at[:, at], out_sem.at[slot])

    steps = out.shape[1] // wide

    @pl.loop(0, steps)
    def _(step):
        slot = step % 2

        @pl.when(step >= 2)
        def _():
            write(step - 2, slot).wait()

        halves = []
        for i in range(row_tiles):
            lhs = left[first + i].reshape(n_q * tile, tile)
            block = amp[i * tile : (i + 1) * tile, pl.ds(pl.multiple_of(step * wide, wide), wide)]
            half = jnp.dot(lhs, block, preferred_element_type=jnp.float32)
            halves.append(half.astype(jnp.bfloat16))
        for j in range(wide // tile):
            col = step * (wide // tile) + j
            cols = slice(j * tile, (j + 1) * tile)
            lhs = jnp.concatenate(
                [
                    jnp.concatenate(
                        [h[q * tile : (q + 1) * tile, cols] for q in range(n_q)], axis=1
                    )
                    for h in halves
                ],
                axis=0,
            )
            rhs = jnp.concatenate([left[col, q] for q in range(n_q)], axis=1)
            acc = lax.dot_general(
                lhs, rhs, (((1,), (1,)), ((), ())), preferred_element_type=jnp.float32
            )
            col_e = virt[pl.ds(screening[pair_id, col], 1), :] - occ[1]
            for i in range(row_tiles):
                rows = slice(i * tile, (i + 1) * tile)
                held[slot, rows, cols] = acc[rows] / (row_den[i] + col_e)
        write(step, slot).start()

    for step in range(max(0, steps - 2), steps):
        write(step, step % 2).wait()


def ladder(screening, tile_slot, occ, virt, amp, mine, other, dims):
    _, _, row_tiles, _, n_q, tile, wide = dims
    rows, columns = amp.shape
    return pl.pallas_call(
        functools.partial(ladder_kernel, dims),
        out_shape=jax.ShapeDtypeStruct((rows, columns), jnp.float32),
        in_specs=[SMEM, SMEM, SMEM, VMEM, VMEM] + [ANY] * 6,
        out_specs=ANY,
        scratch_shapes=[
            pltpu.VMEM((screening.shape[1], n_q, tile, tile), jnp.bfloat16),
            pltpu.VMEM((row_tiles, tile, tile), jnp.float32),
            pltpu.VMEM((2, rows, wide), jnp.float32),
            pltpu.SemaphoreType.DMA,
            pltpu.SemaphoreType.DMA((2,)),
        ],
        compiler_params=pltpu.CompilerParams(vmem_limit_bytes=24 * 2**20),
        name="ladder",
    )(screening, tile_slot, occ, virt, amp, *mine, *other)


def direct(
    amplitudes, factors, screening, tile_slot, pair_orbitals, occupied_energy, virtual_energy
):
    tile_dev, q_cut, tile, _ = factors.shape
    n_pair, n_cut = lax.axis_size("pair"), lax.axis_size("cuts")
    group = n_pair // screening.shape[0]
    shifts = n_pair // group
    row_tiles = amplitudes.shape[0] // tile // n_cut
    me = lax.axis_index("pair")

    def send(x, move):
        pairs = [
            (p * n_cut + c, dst[0] * n_cut + dst[1])
            for p in range(n_pair)
            for c in range(n_cut)
            for dst in [move(p, c)]
        ]
        return lax.ppermute(x, BOTH, pairs)

    picked = pick(screening, tile_slot, factors, group, shifts)
    got = [picked[0]] + [None] * (shifts - 1)
    for s in range(1, shifts):
        got[s] = send(picked[s], lambda p, c: (p ^ (s * group), c))
    crossed = []
    for s in range(shifts):
        crossed.append(send(got[s], lambda p, c: (p, c ^ 1)))
    half = shifts // 2
    mine = [
        jnp.stack(got[:half] + crossed[:half]),
        jnp.stack(got[half:]),
        jnp.stack(crossed[half:]),
    ]
    other = []
    for x in mine:
        other.append(send(x, lambda p, c: (p ^ 1, c)))
    occ = occupied_energy[pair_orbitals[me // group]]
    rows = row_tiles * tile
    amp = lax.dynamic_slice_in_dim(amplitudes, lax.axis_index("cuts") * rows, rows, 0)
    dims = (tile_dev, group, row_tiles, shifts, q_cut * n_cut, tile, 2 * tile)
    return ladder(screening, tile_slot, occ, virtual_energy, amp, mine, other, dims)


def general(
    amplitudes, factors, screening, tile_slot, pair_orbitals, occupied_energy, virtual_energy
):
    tile_dev, q_cut, tile, _ = factors.shape
    count = screening.shape[1]
    me = lax.axis_index("pair")
    row_tiles = amplitudes.shape[0] // tile
    first_tile = me * row_tiles
    pair_id, tile_start = first_tile // count, first_tile % count
    my_tiles = screening[pair_id]
    my_slots = tile_slot[my_tiles]
    device_pairs = jnp.arange(lax.axis_size("pair"), dtype=jnp.int32) * row_tiles // count
    slot_table = tile_slot[screening[device_pairs]]
    wanted = slot_table // tile_dev == me
    local = jnp.sum(jnp.where(wanted, slot_table % tile_dev, 0), axis=1)
    needed = jnp.any(wanted, axis=1)
    outgoing = jnp.where(
        needed[:, None, None, None], factors[local], jnp.zeros((), factors.dtype)
    )
    incoming = lax.all_to_all(outgoing, "pair", split_axis=0, concat_axis=0, tiled=True)
    chosen = incoming[my_slots // tile_dev]
    left = lax.dynamic_slice_in_dim(chosen, tile_start, row_tiles, 0)
    blocks = amplitudes.reshape(row_tiles, tile, count * tile)
    total = jnp.zeros((row_tiles, tile, count, tile), jnp.float32)
    for q in range(q_cut):
        half = jnp.einsum(
            "iac,icx->iax", left[:, q], blocks, preferred_element_type=jnp.float32
        )
        half = half.astype(jnp.bfloat16).reshape(row_tiles, tile, count, tile)
        total = total + jnp.einsum(
            "iajd,jbd->iajb", half, chosen[:, q], preferred_element_type=jnp.float32
        )
    partial = total.reshape(row_tiles * tile, count * tile).astype(jnp.bfloat16)
    summed = lax.psum_scatter(partial, "cuts", scatter_dimension=0, tiled=True)
    occ = occupied_energy[pair_orbitals[pair_id]]
    energy = virtual_energy[my_tiles].reshape(count * tile)
    rows = summed.shape[0]
    begin = tile_start * tile + lax.axis_index("cuts") * rows
    row_energy = lax.dynamic_slice_in_dim(energy - occ[0], begin, rows, 0)
    return summed.astype(jnp.float32) / (row_energy[:, None] + (energy - occ[1])[None, :])


def solution(mesh):
    n_pair, n_cut = mesh.shape["pair"], mesh.shape["cuts"]

    def build(body):
        return jax.shard_map(
            body,
            mesh=mesh,
            in_specs=(P("pair", None), P("pair", "cuts", None, None), P(), P(), P(), P(), P()),
            out_specs=P(BOTH, None),
            check_vma=False,
        )

    def whole(amplitudes, factors, screening, *rest):
        n_pos, count = screening.shape
        every_owner = count == n_pair and n_pair == 2 * n_pos and n_pos & (n_pos - 1) == 0
        if not (every_owner and n_cut == 2):
            return build(general)(amplitudes, factors, screening, *rest)
        step = build(direct)
        return step(amplitudes, factors, screening, *rest)

    return whole
```

```python
import functools

import jax
import jax.numpy as jnp
from jax import lax
from jax.experimental import pallas as pl
from jax.experimental.pallas import tpu as pltpu
from jax.sharding import PartitionSpec as P


BOTH = ("pair", "cuts")
ANY = pl.BlockSpec(memory_space=pl.ANY)
SMEM = pl.BlockSpec(memory_space=pltpu.SMEM)
VMEM = pl.BlockSpec(memory_space=pltpu.VMEM)


def pick_kernel(tile_dev, group, screening, tile_slot, factors, *outs):
    count = screening.shape[1]
    me = lax.axis_index("pair")
    for shift, out in enumerate(outs):
        peer = (me // group) ^ shift
        local = jnp.int32(0)
        for t in range(count):
            slot = tile_slot[screening[peer, t]]
            local = jnp.where(slot // tile_dev == me, slot % tile_dev, local)
        out[...] = factors[local]


def pick(screening, tile_slot, factors, group, shifts):
    tile_dev, *tail = factors.shape
    return pl.pallas_call(
        functools.partial(pick_kernel, tile_dev, group),
        out_shape=[jax.ShapeDtypeStruct(tail, factors.dtype)] * shifts,
        in_specs=[SMEM, SMEM, VMEM],
        out_specs=[VMEM] * shifts,
        compiler_params=pltpu.CompilerParams(vmem_limit_bytes=8 * 2**20),
        name="pick",
    )(screening, tile_slot, factors)


def ladder_kernel(dims, last, screening, tile_slot, occ, virt, amp, *refs):
    tile_dev, group, row_tiles, shifts, tile, wide = dims
    (near, far, near_other, far_other), refs = refs[:4], refs[4:]
    if last:
        before, out, left, row_den, held, out_sem = refs
    else:
        out, left = refs
    me, cut = lax.axis_index("pair"), lax.axis_index("cuts")
    pair_id, core = me // group, me % group
    count, n_q = screening.shape[1], left.shape[1]
    first = core * (count // group) + cut * row_tiles
    half = shifts // 2

    for t in range(count):
        slot = tile_slot[screening[pair_id, t]]
        owner = slot // tile_dev
        shift = (owner // group) ^ pair_id
        same = owner % group == core
        close = shift < half
        for bufs, held_by in (((near, far), same), ((near_other, far_other), jnp.logical_not(same))):

            @pl.when(held_by & close)
            def _():
                left[t] = bufs[0][shift]

            @pl.when(held_by & jnp.logical_not(close))
            def _():
                left[t] = bufs[1][shift - half]

    if last:
        for i in range(row_tiles):
            row = virt[pl.ds(screening[pair_id, first + i], 1), :] - occ[0]
            row_den[i] = jnp.broadcast_to(row, (tile, tile)).T

    def write(step, slot):
        at = pl.ds(pl.multiple_of(step * wide, wide), wide)
        return pltpu.make_async_copy(held.at[slot], out.at[:, at], out_sem.at[slot])

    steps = out.shape[1] // wide

    @pl.loop(0, steps)
    def _(step):
        slot = step % 2
        base = pl.multiple_of(step * wide, wide)

        if last:

            @pl.when(step >= 2)
            def _():
                write(step - 2, slot).wait()

        halves = []
        for i in range(row_tiles):
            lhs = left[first + i].reshape(n_q * tile, tile)
            block = amp[i * tile : (i + 1) * tile, pl.ds(base, wide)]
            half_done = jnp.dot(lhs, block, preferred_element_type=jnp.float32)
            halves.append(half_done.astype(jnp.bfloat16))
        for j in range(wide // tile):
            col = step * (wide // tile) + j
            cols = slice(j * tile, (j + 1) * tile)
            lhs = jnp.concatenate(
                [
                    jnp.concatenate(
                        [h[q * tile : (q + 1) * tile, cols] for q in range(n_q)], axis=1
                    )
                    for h in halves
                ],
                axis=0,
            )
            rhs = jnp.concatenate([left[col, q] for q in range(n_q)], axis=1)
            acc = lax.dot_general(
                lhs, rhs, (((1,), (1,)), ((), ())), preferred_element_type=jnp.float32
            )
            at = pl.ds(pl.multiple_of(base + j * tile, tile), tile)
            if not last:
                out[:, at] = acc
                continue
            acc = acc + before[:, at]
            col_e = virt[pl.ds(screening[pair_id, col], 1), :] - occ[1]
            for i in range(row_tiles):
                rows = slice(i * tile, (i + 1) * tile)
                held[slot, rows, cols] = acc[rows] / (row_den[i] + col_e)
        if last:
            write(step, slot).start()

    if last:
        for step in range(max(0, steps - 2), steps):
            write(step, step % 2).wait()


def ladder(screening, tile_slot, occ, virt, amp, tiles, dims, before=None):
    _, _, row_tiles, _, tile, wide = dims
    rows, columns = amp.shape
    last = before is not None
    n_q = tiles[0].shape[1]
    scratch = [pltpu.VMEM((screening.shape[1], n_q, tile, tile), jnp.bfloat16)]
    if last:
        scratch += [
            pltpu.VMEM((row_tiles, tile, tile), jnp.float32),
            pltpu.VMEM((2, rows, wide), jnp.float32),
            pltpu.SemaphoreType.DMA((2,)),
        ]
    extra = [before] if last else []
    flops = 4 * n_q * rows * columns * tile
    return pl.pallas_call(
        functools.partial(ladder_kernel, dims, last),
        out_shape=jax.ShapeDtypeStruct((rows, columns), jnp.float32),
        in_specs=[SMEM, SMEM, SMEM] + [VMEM] * (6 + len(extra)),
        out_specs=ANY if last else VMEM,
        scratch_shapes=scratch,
        compiler_params=pltpu.CompilerParams(vmem_limit_bytes=(16 if last else 12) * 2**20),
        cost_estimate=pl.CostEstimate(flops=flops, bytes_accessed=0, transcendentals=0),
        name="ladder_last" if last else "ladder_first",
    )(screening, tile_slot, occ, virt, amp, *tiles, *extra)


def crossings(shifts):
    near = [[s, s + 1] for s in range(2, shifts // 2, 2)]
    far = [[s, s + 1] for s in range(shifts // 2, shifts, 2)]
    groups = [[0], [1]]
    while near or far:
        groups += [x.pop(0) for x in (far, near) if x and (x is near or len(x) > 1 or not near)]
    return groups


def direct(
    amplitudes, factors, screening, tile_slot, pair_orbitals, occupied_energy, virtual_energy
):
    tile_dev, _, tile, _ = factors.shape
    n_pair, n_cut = lax.axis_size("pair"), lax.axis_size("cuts")
    group = n_pair // screening.shape[0]
    shifts = n_pair // group
    half = shifts // 2
    row_tiles = amplitudes.shape[0] // tile // n_cut
    me = lax.axis_index("pair")

    def send(x, move):
        pairs = [
            (p * n_cut + c, dst[0] * n_cut + dst[1])
            for p in range(n_pair)
            for c in range(n_cut)
            for dst in [move(p, c)]
        ]
        return lax.ppermute(x, BOTH, pairs)

    def over(x):
        return send(x, lambda p, c: (p ^ 1, c))

    picked = pick(screening, tile_slot, factors, group, shifts)
    got = [picked[0]] + [
        send(picked[s], lambda p, c: (p ^ (s * group), c))
        for s in range(1, shifts)
    ]
    crossed = [None] * shifts
    for members in crossings(shifts):
        x = jnp.stack([got[s] for s in members])
        x = send(x, lambda p, c: (p, c ^ 1))
        for n, s in enumerate(members):
            crossed[s] = x[n]
    occ = occupied_energy[pair_orbitals[me // group]]
    rows = row_tiles * tile
    amp = lax.dynamic_slice_in_dim(amplitudes, lax.axis_index("cuts") * rows, rows, 0)
    dims = (tile_dev, group, row_tiles, shifts, tile, 2 * tile)
    out = None
    for held in (got, crossed):
        near = jnp.stack(held[:half])
        far = jnp.stack(held[half:])
        tiles = [near, far, over(near), over(far)]
        out = ladder(screening, tile_slot, occ, virtual_energy, amp, tiles, dims, out)
    return out


def general(
    amplitudes, factors, screening, tile_slot, pair_orbitals, occupied_energy, virtual_energy
):
    tile_dev, q_cut, tile, _ = factors.shape
    count = screening.shape[1]
    me = lax.axis_index("pair")
    row_tiles = amplitudes.shape[0] // tile
    first_tile = me * row_tiles
    pair_id, tile_start = first_tile // count, first_tile % count
    my_tiles = screening[pair_id]
    my_slots = tile_slot[my_tiles]
    device_pairs = jnp.arange(lax.axis_size("pair"), dtype=jnp.int32) * row_tiles // count
    slot_table = tile_slot[screening[device_pairs]]
    wanted = slot_table // tile_dev == me
    local = jnp.sum(jnp.where(wanted, slot_table % tile_dev, 0), axis=1)
    needed = jnp.any(wanted, axis=1)
    outgoing = jnp.where(
        needed[:, None, None, None], factors[local], jnp.zeros((), factors.dtype)
    )
    incoming = lax.all_to_all(outgoing, "pair", split_axis=0, concat_axis=0, tiled=True)
    chosen = incoming[my_slots // tile_dev]
    left = lax.dynamic_slice_in_dim(chosen, tile_start, row_tiles, 0)
    blocks = amplitudes.reshape(row_tiles, tile, count * tile)
    total = jnp.zeros((row_tiles, tile, count, tile), jnp.float32)
    for q in range(q_cut):
        half = jnp.einsum(
            "iac,icx->iax", left[:, q], blocks, preferred_element_type=jnp.float32
        )
        half = half.astype(jnp.bfloat16).reshape(row_tiles, tile, count, tile)
        total = total + jnp.einsum(
            "iajd,jbd->iajb", half, chosen[:, q], preferred_element_type=jnp.float32
        )
    partial = total.reshape(row_tiles * tile, count * tile).astype(jnp.bfloat16)
    summed = lax.psum_scatter(partial, "cuts", scatter_dimension=0, tiled=True)
    occ = occupied_energy[pair_orbitals[pair_id]]
    energy = virtual_energy[my_tiles].reshape(count * tile)
    rows = summed.shape[0]
    begin = tile_start * tile + lax.axis_index("cuts") * rows
    row_energy = lax.dynamic_slice_in_dim(energy - occ[0], begin, rows, 0)
    return summed.astype(jnp.float32) / (row_energy[:, None] + (energy - occ[1])[None, :])


def solution(mesh):
    n_pair, n_cut = mesh.shape["pair"], mesh.shape["cuts"]

    def build(body):
        return jax.shard_map(
            body,
            mesh=mesh,
            in_specs=(P("pair", None), P("pair", "cuts", None, None), P(), P(), P(), P(), P()),
            out_specs=P(BOTH, None),
            check_vma=False,
        )

    def whole(amplitudes, factors, screening, *rest):
        n_pos, count = screening.shape
        every_owner = count == n_pair and n_pair == 2 * n_pos and n_pos & (n_pos - 1) == 0
        if not (every_owner and n_cut == 2):
            return build(general)(amplitudes, factors, screening, *rest)
        step = build(direct)
        return step(amplitudes, factors, screening, *rest)

    return whole
```

```python
import functools

import jax
import jax.numpy as jnp
from jax import lax
from jax.experimental import pallas as pl
from jax.experimental.pallas import tpu as pltpu
from jax.sharding import PartitionSpec as P


BOTH = ("pair", "cuts")
ANY = pl.BlockSpec(memory_space=pl.ANY)
SMEM = pl.BlockSpec(memory_space=pltpu.SMEM)
VMEM = pl.BlockSpec(memory_space=pltpu.VMEM)


def pick_kernel(tile_dev, group, screening, tile_slot, factors, *refs):
    *outs, shown, slots, held, sems = refs
    copies = [
        pltpu.make_async_copy(screening, shown, sems.at[0]),
        pltpu.make_async_copy(tile_slot, slots, sems.at[1]),
        pltpu.make_async_copy(factors, held, sems.at[2]),
    ]
    for copy in copies:
        copy.start()
    me = lax.axis_index("pair")
    copies[1].wait()
    tiles = [jnp.int32(0)] * tile_dev
    for t in range(tile_slot.shape[0]):
        slot = slots[t]
        tiles = [jnp.where(slot == me * tile_dev + n, t, x) for n, x in enumerate(tiles)]
    copies[0].wait()
    local = []
    for shift in range(len(outs)):
        peer = (me // group) ^ shift
        found = jnp.int32(0)
        for t in range(screening.shape[1]):
            tile = shown[peer, t]
            for n in range(1, tile_dev):
                found = jnp.where(tile == tiles[n], n, found)
        local.append(found)
    copies[2].wait()
    copies = [
        pltpu.make_async_copy(held.at[found], out, sems.at[3 + n])
        for n, (out, found) in enumerate(zip(outs, local))
    ]
    for copy in copies:
        copy.start()
    for copy in copies:
        copy.wait()


def pick(screening, tile_slot, factors, group, shifts):
    tile_dev, *tail = factors.shape
    hbm = pl.BlockSpec(memory_space=pltpu.HBM)
    return pl.pallas_call(
        functools.partial(pick_kernel, tile_dev, group),
        out_shape=[jax.ShapeDtypeStruct(tail, factors.dtype)] * shifts,
        in_specs=[hbm, hbm, hbm],
        out_specs=[ANY] * shifts,
        scratch_shapes=[
            pltpu.SMEM(screening.shape, jnp.int32),
            pltpu.SMEM(tile_slot.shape, jnp.int32),
            pltpu.VMEM(factors.shape, factors.dtype),
            pltpu.SemaphoreType.DMA((3 + shifts,)),
        ],
        name="pick",
    )(screening, tile_slot, factors)


def ladder_kernel(dims, last, screening, tile_slot, occ, virt, amp, *refs):
    tile_dev, group, row_tiles, shifts, tile = dims
    bufs, refs = refs[:4], refs[4:]
    if last:
        before, out, left, place, row_den, held, sems = refs
    else:
        out, left, place = refs
    me, cut = lax.axis_index("pair"), lax.axis_index("cuts")
    pair_id, core = me // group, me % group
    count, n_q = screening.shape[1], left.shape[1]
    first = core * (count // group) + cut * row_tiles
    half = shifts // 2

    for t in range(count):
        slot = tile_slot[screening[pair_id, t]]
        owner = slot // tile_dev
        shift = (owner // group) ^ pair_id
        place[shift + (owner % group ^ core) * shifts] = t
    for i in range(row_tiles):
        slot = tile_slot[screening[pair_id, first + i]]
        owner = slot // tile_dev
        shift = (owner // group) ^ pair_id
        which = shift // half + (owner % group ^ core) * 2
        for n, buf in enumerate(bufs):

            @pl.when(which == n)
            def _():
                left[i] = buf[shift % half]

        if last:
            row = virt[pl.ds(screening[pair_id, first + i], 1), :] - occ[0]
            row_den[i] = jnp.broadcast_to(row, (tile, tile)).T

    writes = []
    for source in range(0, count, 2):
        pair = [(n, bufs[n // half][n % half], place[n]) for n in (source, source + 1)]
        offsets = [pl.multiple_of(at * tile, tile) for _, _, at in pair]
        halves = []
        for i in range(row_tiles):
            rows = slice(i * tile, (i + 1) * tile)
            block = jnp.concatenate([amp[rows, pl.ds(x, tile)] for x in offsets], axis=1)
            lhs = left[i].reshape(n_q * tile, tile)
            half_done = jnp.dot(lhs, block, preferred_element_type=jnp.float32)
            halves.append(half_done.astype(jnp.bfloat16))
        for j, (n, tiles, at) in enumerate(pair):
            cols = slice(j * tile, (j + 1) * tile)
            lhs = jnp.concatenate(
                [
                    jnp.concatenate(
                        [h[q * tile : (q + 1) * tile, cols] for q in range(n_q)], axis=1
                    )
                    for h in halves
                ],
                axis=0,
            )
            rhs = jnp.concatenate([tiles[q] for q in range(n_q)], axis=1)
            acc = lax.dot_general(
                lhs, rhs, (((1,), (1,)), ((), ())), preferred_element_type=jnp.float32
            )
            if not last:
                out[n] = acc
                continue
            acc = acc + before[n]
            col_e = virt[pl.ds(screening[pair_id, at], 1), :] - occ[1]
            for i in range(row_tiles):
                rows = slice(i * tile, (i + 1) * tile)
                held[n, rows, :] = acc[rows] / (row_den[i] + col_e)
            copy = pltpu.make_async_copy(held.at[n], out.at[:, pl.ds(offsets[j], tile)], sems.at[n])
            copy.start()
            writes.append(copy)
    for copy in writes:
        copy.wait()


def ladder(screening, tile_slot, occ, virt, amp, tiles, dims, before=None):
    _, _, row_tiles, _, tile = dims
    count, columns = screening.shape[1], amp.shape[1]
    rows = row_tiles * tile
    last = before is not None
    n_q = tiles[0].shape[1]
    scratch = [
        pltpu.VMEM((row_tiles, n_q, tile, tile), jnp.bfloat16),
        pltpu.SMEM((count,), jnp.int32),
    ]
    if last:
        scratch += [
            pltpu.VMEM((row_tiles, tile, tile), jnp.float32),
            pltpu.VMEM((count, rows, tile), jnp.float32),
            pltpu.SemaphoreType.DMA((count,)),
        ]
        out = jax.ShapeDtypeStruct((rows, columns), jnp.float32)
    else:
        out = jax.ShapeDtypeStruct((count, rows, tile), jnp.float32)
    extra = [before] if last else []
    flops = 4 * n_q * rows * columns * tile
    return pl.pallas_call(
        functools.partial(ladder_kernel, dims, last),
        out_shape=out,
        in_specs=[SMEM, SMEM, SMEM] + [VMEM] * (6 + len(extra)),
        out_specs=ANY if last else VMEM,
        scratch_shapes=scratch,
        compiler_params=pltpu.CompilerParams(vmem_limit_bytes=26 * 2**20),
        cost_estimate=pl.CostEstimate(flops=flops, bytes_accessed=0, transcendentals=0),
        name="ladder_last" if last else "ladder_first",
    )(screening, tile_slot, occ, virt, amp, *tiles, *extra)


def crossings(shifts):
    near = [[s, s + 1] for s in range(2, shifts // 2, 2)]
    far = [[s, s + 1] for s in range(shifts // 2, shifts, 2)]
    groups = [[0], [1]]
    while near or far:
        groups += [x.pop(0) for x in (far, near) if x and (x is near or len(x) > 1 or not near)]
    return groups


def direct(
    amplitudes, factors, screening, tile_slot, pair_orbitals, occupied_energy, virtual_energy
):
    tile_dev, _, tile, _ = factors.shape
    n_pair, n_cut = lax.axis_size("pair"), lax.axis_size("cuts")
    group = n_pair // screening.shape[0]
    shifts = n_pair // group
    half = shifts // 2
    row_tiles = amplitudes.shape[0] // tile // n_cut
    me = lax.axis_index("pair")

    def send(x, move):
        pairs = [
            (p * n_cut + c, dst[0] * n_cut + dst[1])
            for p in range(n_pair)
            for c in range(n_cut)
            for dst in [move(p, c)]
        ]
        return lax.ppermute(x, BOTH, pairs)

    def over(x):
        return send(x, lambda p, c: (p ^ 1, c))

    picked = pick(screening, tile_slot, factors, group, shifts)
    got = [picked[0]] + [
        send(picked[s], lambda p, c: (p ^ (s * group), c))
        for s in range(1, shifts)
    ]
    crossed = [None] * shifts
    for members in crossings(shifts):
        x = jnp.stack([got[s] for s in members])
        x = send(x, lambda p, c: (p, c ^ 1))
        for n, s in enumerate(members):
            crossed[s] = x[n]
    occ = occupied_energy[pair_orbitals[me // group]]
    rows = row_tiles * tile
    amp = lax.dynamic_slice_in_dim(amplitudes, lax.axis_index("cuts") * rows, rows, 0)
    dims = (tile_dev, group, row_tiles, shifts, tile)
    out = None
    for held in (got, crossed):
        near = jnp.stack(held[:half])
        far = jnp.stack(held[half:])
        tiles = [near, far, over(near), over(far)]
        out = ladder(screening, tile_slot, occ, virtual_energy, amp, tiles, dims, out)
    return out


def general(
    amplitudes, factors, screening, tile_slot, pair_orbitals, occupied_energy, virtual_energy
):
    tile_dev, q_cut, tile, _ = factors.shape
    count = screening.shape[1]
    me = lax.axis_index("pair")
    row_tiles = amplitudes.shape[0] // tile
    first_tile = me * row_tiles
    pair_id, tile_start = first_tile // count, first_tile % count
    my_tiles = screening[pair_id]
    my_slots = tile_slot[my_tiles]
    device_pairs = jnp.arange(lax.axis_size("pair"), dtype=jnp.int32) * row_tiles // count
    slot_table = tile_slot[screening[device_pairs]]
    wanted = slot_table // tile_dev == me
    local = jnp.sum(jnp.where(wanted, slot_table % tile_dev, 0), axis=1)
    needed = jnp.any(wanted, axis=1)
    outgoing = jnp.where(
        needed[:, None, None, None], factors[local], jnp.zeros((), factors.dtype)
    )
    incoming = lax.all_to_all(outgoing, "pair", split_axis=0, concat_axis=0, tiled=True)
    chosen = incoming[my_slots // tile_dev]
    left = lax.dynamic_slice_in_dim(chosen, tile_start, row_tiles, 0)
    blocks = amplitudes.reshape(row_tiles, tile, count * tile)
    total = jnp.zeros((row_tiles, tile, count, tile), jnp.float32)
    for q in range(q_cut):
        half = jnp.einsum(
            "iac,icx->iax", left[:, q], blocks, preferred_element_type=jnp.float32
        )
        half = half.astype(jnp.bfloat16).reshape(row_tiles, tile, count, tile)
        total = total + jnp.einsum(
            "iajd,jbd->iajb", half, chosen[:, q], preferred_element_type=jnp.float32
        )
    partial = total.reshape(row_tiles * tile, count * tile).astype(jnp.bfloat16)
    summed = lax.psum_scatter(partial, "cuts", scatter_dimension=0, tiled=True)
    occ = occupied_energy[pair_orbitals[pair_id]]
    energy = virtual_energy[my_tiles].reshape(count * tile)
    rows = summed.shape[0]
    begin = tile_start * tile + lax.axis_index("cuts") * rows
    row_energy = lax.dynamic_slice_in_dim(energy - occ[0], begin, rows, 0)
    return summed.astype(jnp.float32) / (row_energy[:, None] + (energy - occ[1])[None, :])


def solution(mesh):
    n_pair, n_cut = mesh.shape["pair"], mesh.shape["cuts"]

    def build(body):
        return jax.shard_map(
            body,
            mesh=mesh,
            in_specs=(P("pair", None), P("pair", "cuts", None, None), P(), P(), P(), P(), P()),
            out_specs=P(BOTH, None),
            check_vma=False,
        )

    def whole(amplitudes, factors, screening, *rest):
        n_pos, count = screening.shape
        every_owner = count == n_pair and n_pair == 2 * n_pos and n_pos & (n_pos - 1) == 0
        if not (every_owner and n_cut == 2):
            return build(general)(amplitudes, factors, screening, *rest)
        step = build(direct)
        return step(amplitudes, factors, screening, *rest)

    return whole
```

```python
import functools

import jax
import jax.numpy as jnp
from jax import lax
from jax.experimental import pallas as pl
from jax.experimental.pallas import tpu as pltpu
from jax.sharding import PartitionSpec as P


BOTH = ("pair", "cuts")
ANY = pl.BlockSpec(memory_space=pl.ANY)
SMEM = pl.BlockSpec(memory_space=pltpu.SMEM)
VMEM = pl.BlockSpec(memory_space=pltpu.VMEM)


def pick_kernel(tile_dev, group, screening, tile_slot, factors, *refs):
    *outs, shown, slots, held, sems = refs
    copies = [
        pltpu.make_async_copy(screening, shown, sems.at[0]),
        pltpu.make_async_copy(tile_slot, slots, sems.at[1]),
        pltpu.make_async_copy(factors, held, sems.at[2]),
    ]
    for copy in copies:
        copy.start()
    me = lax.axis_index("pair")
    copies[1].wait()
    tiles = [jnp.int32(0)] * tile_dev
    for t in range(tile_slot.shape[0]):
        slot = slots[t]
        tiles = [jnp.where(slot == me * tile_dev + n, t, x) for n, x in enumerate(tiles)]
    copies[0].wait()
    local = []
    for shift in range(len(outs)):
        peer = (me // group) ^ shift
        found = jnp.int32(0)
        for t in range(screening.shape[1]):
            tile = shown[peer, t]
            for n in range(1, tile_dev):
                found = jnp.where(tile == tiles[n], n, found)
        local.append(found)
    copies[2].wait()
    copies = [
        pltpu.make_async_copy(held.at[found], out, sems.at[3 + n])
        for n, (out, found) in enumerate(zip(outs, local))
    ]
    for copy in copies:
        copy.start()
    for copy in copies:
        copy.wait()


def pick(screening, tile_slot, factors, group, shifts):
    tile_dev, *tail = factors.shape
    hbm = pl.BlockSpec(memory_space=pltpu.HBM)
    return pl.pallas_call(
        functools.partial(pick_kernel, tile_dev, group),
        out_shape=[jax.ShapeDtypeStruct(tail, factors.dtype)] * shifts,
        in_specs=[hbm, hbm, hbm],
        out_specs=[ANY] * shifts,
        scratch_shapes=[
            pltpu.SMEM(screening.shape, jnp.int32),
            pltpu.SMEM(tile_slot.shape, jnp.int32),
            pltpu.VMEM(factors.shape, factors.dtype),
            pltpu.SemaphoreType.DMA((3 + shifts,)),
        ],
        name="pick",
    )(screening, tile_slot, factors)


def ladder_kernel(dims, last, screening, tile_slot, occ, virt, amp, *refs):
    tile_dev, group, row_tiles, shifts, tile = dims
    bufs, refs = refs[:4], refs[4:]
    if last:
        before, out, left, place, row_den, held, sems = refs
    else:
        out, left, place = refs
    me, cut = lax.axis_index("pair"), lax.axis_index("cuts")
    pair_id, core = me // group, me % group
    count, n_q = screening.shape[1], left.shape[1]
    first = core * (count // group) + cut * row_tiles
    half = shifts // 2

    for t in range(count):
        slot = tile_slot[screening[pair_id, t]]
        owner = slot // tile_dev
        shift = (owner // group) ^ pair_id
        place[shift + (owner % group ^ core) * shifts] = t
    for i in range(row_tiles):
        slot = tile_slot[screening[pair_id, first + i]]
        owner = slot // tile_dev
        shift = (owner // group) ^ pair_id
        which = shift // half + (owner % group ^ core) * 2
        for n, buf in enumerate(bufs):

            @pl.when(which == n)
            def _():
                left[i] = buf[shift % half]

        if last:
            row = virt[pl.ds(screening[pair_id, first + i], 1), :] - occ[0]
            row_den[i] = jnp.broadcast_to(row, (tile, tile)).T

    writes = []
    for source in range(0, count, 2):
        pair = [(n, bufs[n // half][n % half], place[n]) for n in (source, source + 1)]
        offsets = [pl.multiple_of(at * tile, tile) for _, _, at in pair]
        halves = []
        for i in range(row_tiles):
            rows = slice(i * tile, (i + 1) * tile)
            block = jnp.concatenate([amp[rows, pl.ds(x, tile)] for x in offsets], axis=1)
            lhs = left[i].reshape(n_q * tile, tile)
            half_done = jnp.dot(lhs, block, preferred_element_type=jnp.float32)
            halves.append(half_done.astype(jnp.bfloat16))
        lhs = jnp.concatenate(
            [
                jnp.concatenate([h[q * tile : (q + 1) * tile] for q in range(n_q)], axis=1)
                for h in halves
            ],
            axis=0,
        )
        zero = jnp.zeros((tile, tile), jnp.bfloat16)
        rhs = jnp.concatenate(
            [
                jnp.concatenate(
                    [x for q in range(n_q) for x in ((tiles[q], zero), (zero, tiles[q]))[j]],
                    axis=1,
                )
                for j, (_, tiles, _) in enumerate(pair)
            ],
            axis=0,
        )
        both = lax.dot_general(
            lhs, rhs, (((1,), (1,)), ((), ())), preferred_element_type=jnp.float32
        )
        for j, (n, _, at) in enumerate(pair):
            acc = both[:, j * tile : (j + 1) * tile]
            if not last:
                out[n] = acc
                continue
            acc = acc + before[n]
            col_e = virt[pl.ds(screening[pair_id, at], 1), :] - occ[1]
            for i in range(row_tiles):
                rows = slice(i * tile, (i + 1) * tile)
                held[n, rows, :] = acc[rows] / (row_den[i] + col_e)
            copy = pltpu.make_async_copy(held.at[n], out.at[:, pl.ds(offsets[j], tile)], sems.at[n])
            copy.start()
            writes.append(copy)
    for copy in writes:
        copy.wait()


def ladder(screening, tile_slot, occ, virt, amp, tiles, dims, before=None):
    _, _, row_tiles, _, tile = dims
    count, columns = screening.shape[1], amp.shape[1]
    rows = row_tiles * tile
    last = before is not None
    n_q = tiles[0].shape[1]
    scratch = [
        pltpu.VMEM((row_tiles, n_q, tile, tile), jnp.bfloat16),
        pltpu.SMEM((count,), jnp.int32),
    ]
    if last:
        scratch += [
            pltpu.VMEM((row_tiles, tile, tile), jnp.float32),
            pltpu.VMEM((count, rows, tile), jnp.float32),
            pltpu.SemaphoreType.DMA((count,)),
        ]
        out = jax.ShapeDtypeStruct((rows, columns), jnp.float32)
    else:
        out = jax.ShapeDtypeStruct((count, rows, tile), jnp.float32)
    extra = [before] if last else []
    flops = 4 * n_q * rows * columns * tile
    return pl.pallas_call(
        functools.partial(ladder_kernel, dims, last),
        out_shape=out,
        in_specs=[SMEM, SMEM, SMEM] + [VMEM] * (6 + len(extra)),
        out_specs=ANY if last else VMEM,
        scratch_shapes=scratch,
        compiler_params=pltpu.CompilerParams(vmem_limit_bytes=26 * 2**20),
        cost_estimate=pl.CostEstimate(flops=flops, bytes_accessed=0, transcendentals=0),
        name="ladder_last" if last else "ladder_first",
    )(screening, tile_slot, occ, virt, amp, *tiles, *extra)


def crossings(shifts):
    half = shifts // 2
    early = [[s] for s in (0, 1, half, half + 1)]
    near = [[s, s + 1] for s in range(2, half, 2)]
    return early + near + [[s] for s in range(half + 2, shifts)]


def direct(
    amplitudes, factors, screening, tile_slot, pair_orbitals, occupied_energy, virtual_energy
):
    tile_dev, _, tile, _ = factors.shape
    n_pair, n_cut = lax.axis_size("pair"), lax.axis_size("cuts")
    group = n_pair // screening.shape[0]
    shifts = n_pair // group
    half = shifts // 2
    row_tiles = amplitudes.shape[0] // tile // n_cut
    me = lax.axis_index("pair")

    def send(x, move):
        pairs = [
            (p * n_cut + c, dst[0] * n_cut + dst[1])
            for p in range(n_pair)
            for c in range(n_cut)
            for dst in [move(p, c)]
        ]
        return lax.ppermute(x, BOTH, pairs)

    def over(x):
        return send(x, lambda p, c: (p ^ 1, c))

    picked = pick(screening, tile_slot, factors, group, shifts)
    got = [picked[0]] + [
        send(picked[s], lambda p, c: (p ^ (s * group), c))
        for s in range(1, shifts)
    ]
    crossed = [None] * shifts
    for members in crossings(shifts):
        x = got[members[0]]
        if len(members) > 1:
            x = jnp.stack([got[s] for s in members])
        x = send(x, lambda p, c: (p, c ^ 1))
        for n, s in enumerate(members):
            crossed[s] = x[n] if len(members) > 1 else x
    occ = occupied_energy[pair_orbitals[me // group]]
    rows = row_tiles * tile
    amp = lax.dynamic_slice_in_dim(amplitudes, lax.axis_index("cuts") * rows, rows, 0)
    dims = (tile_dev, group, row_tiles, shifts, tile)
    out = None
    for held in (got, crossed):
        near = jnp.stack(held[:half])
        far = jnp.stack(held[half:])
        tiles = [near, far, over(near), over(far)]
        out = ladder(screening, tile_slot, occ, virtual_energy, amp, tiles, dims, out)
    return out


def general(
    amplitudes, factors, screening, tile_slot, pair_orbitals, occupied_energy, virtual_energy
):
    tile_dev, q_cut, tile, _ = factors.shape
    count = screening.shape[1]
    me = lax.axis_index("pair")
    row_tiles = amplitudes.shape[0] // tile
    first_tile = me * row_tiles
    pair_id, tile_start = first_tile // count, first_tile % count
    my_tiles = screening[pair_id]
    my_slots = tile_slot[my_tiles]
    device_pairs = jnp.arange(lax.axis_size("pair"), dtype=jnp.int32) * row_tiles // count
    slot_table = tile_slot[screening[device_pairs]]
    wanted = slot_table // tile_dev == me
    local = jnp.sum(jnp.where(wanted, slot_table % tile_dev, 0), axis=1)
    needed = jnp.any(wanted, axis=1)
    outgoing = jnp.where(
        needed[:, None, None, None], factors[local], jnp.zeros((), factors.dtype)
    )
    incoming = lax.all_to_all(outgoing, "pair", split_axis=0, concat_axis=0, tiled=True)
    chosen = incoming[my_slots // tile_dev]
    left = lax.dynamic_slice_in_dim(chosen, tile_start, row_tiles, 0)
    blocks = amplitudes.reshape(row_tiles, tile, count * tile)
    total = jnp.zeros((row_tiles, tile, count, tile), jnp.float32)
    for q in range(q_cut):
        half = jnp.einsum(
            "iac,icx->iax", left[:, q], blocks, preferred_element_type=jnp.float32
        )
        half = half.astype(jnp.bfloat16).reshape(row_tiles, tile, count, tile)
        total = total + jnp.einsum(
            "iajd,jbd->iajb", half, chosen[:, q], preferred_element_type=jnp.float32
        )
    partial = total.reshape(row_tiles * tile, count * tile).astype(jnp.bfloat16)
    summed = lax.psum_scatter(partial, "cuts", scatter_dimension=0, tiled=True)
    occ = occupied_energy[pair_orbitals[pair_id]]
    energy = virtual_energy[my_tiles].reshape(count * tile)
    rows = summed.shape[0]
    begin = tile_start * tile + lax.axis_index("cuts") * rows
    row_energy = lax.dynamic_slice_in_dim(energy - occ[0], begin, rows, 0)
    return summed.astype(jnp.float32) / (row_energy[:, None] + (energy - occ[1])[None, :])


def solution(mesh):
    n_pair, n_cut = mesh.shape["pair"], mesh.shape["cuts"]

    def build(body):
        return jax.shard_map(
            body,
            mesh=mesh,
            in_specs=(P("pair", None), P("pair", "cuts", None, None), P(), P(), P(), P(), P()),
            out_specs=P(BOTH, None),
            check_vma=False,
        )

    def whole(amplitudes, factors, screening, *rest):
        n_pos, count = screening.shape
        every_owner = count == n_pair and n_pair == 2 * n_pos and n_pos & (n_pos - 1) == 0
        if not (every_owner and n_cut == 2):
            return build(general)(amplitudes, factors, screening, *rest)
        step = build(direct)
        return step(amplitudes, factors, screening, *rest)

    return whole
```

```python
import functools

import jax
import jax.numpy as jnp
from jax import lax
from jax.experimental import pallas as pl
from jax.experimental.pallas import tpu as pltpu
from jax.sharding import PartitionSpec as P


BOTH = ("pair", "cuts")
ANY = pl.BlockSpec(memory_space=pl.ANY)
SMEM = pl.BlockSpec(memory_space=pltpu.SMEM)
VMEM = pl.BlockSpec(memory_space=pltpu.VMEM)


def pick_kernel(tile_dev, group, screening, tile_slot, factors, *refs):
    *outs, shown, slots, held, sems = refs
    copies = [
        pltpu.make_async_copy(screening, shown, sems.at[0]),
        pltpu.make_async_copy(tile_slot, slots, sems.at[1]),
        pltpu.make_async_copy(factors, held, sems.at[2]),
    ]
    for copy in copies:
        copy.start()
    me = lax.axis_index("pair")
    copies[1].wait()
    tiles = [jnp.int32(0)] * tile_dev
    for t in range(tile_slot.shape[0]):
        slot = slots[t]
        tiles = [jnp.where(slot == me * tile_dev + n, t, x) for n, x in enumerate(tiles)]
    copies[0].wait()
    local = []
    for shift in range(len(outs)):
        peer = (me // group) ^ shift
        found = jnp.int32(0)
        for t in range(screening.shape[1]):
            tile = shown[peer, t]
            for n in range(1, tile_dev):
                found = jnp.where(tile == tiles[n], n, found)
        local.append(found)
    copies[2].wait()
    copies = [
        pltpu.make_async_copy(held.at[found], out, sems.at[3 + n])
        for n, (out, found) in enumerate(zip(outs, local))
    ]
    for copy in copies:
        copy.start()
    for copy in copies:
        copy.wait()


def pick(screening, tile_slot, factors, group, shifts):
    tile_dev, *tail = factors.shape
    hbm = pl.BlockSpec(memory_space=pltpu.HBM)
    return pl.pallas_call(
        functools.partial(pick_kernel, tile_dev, group),
        out_shape=[jax.ShapeDtypeStruct(tail, factors.dtype)] * shifts,
        in_specs=[hbm, hbm, hbm],
        out_specs=[ANY] * shifts,
        scratch_shapes=[
            pltpu.SMEM(screening.shape, jnp.int32),
            pltpu.SMEM(tile_slot.shape, jnp.int32),
            pltpu.VMEM(factors.shape, factors.dtype),
            pltpu.SemaphoreType.DMA((3 + shifts,)),
        ],
        name="pick",
    )(screening, tile_slot, factors)


def plan_kernel(dims, screening, tile_slot, occ, virt, table, row_den, col_e):
    tile_dev, group, row_tiles, shifts, tile = dims
    me, cut = lax.axis_index("pair"), lax.axis_index("cuts")
    pair_id, core = me // group, me % group
    count = screening.shape[1]
    first = core * (count // group) + cut * row_tiles

    def source(t):
        slot = tile_slot[screening[pair_id, t]]
        owner = slot // tile_dev
        shift = (owner // group) ^ pair_id
        return shift + (owner % group ^ core) * shifts

    for t in range(count):
        n = source(t)
        table[n] = t
        col_e[pl.ds(n, 1), :] = virt[pl.ds(screening[pair_id, t], 1), :] - occ[1]
    for i in range(row_tiles):
        table[count + i] = source(first + i)
        row = virt[pl.ds(screening[pair_id, first + i], 1), :] - occ[0]
        row_den[i] = jnp.broadcast_to(row, (tile, tile)).T


def plan(screening, tile_slot, occ, virt, dims):
    _, _, row_tiles, _, tile = dims
    count = screening.shape[1]
    return pl.pallas_call(
        functools.partial(plan_kernel, dims),
        out_shape=[
            jax.ShapeDtypeStruct((count + row_tiles,), jnp.int32),
            jax.ShapeDtypeStruct((row_tiles, tile, tile), jnp.float32),
            jax.ShapeDtypeStruct((count, tile), jnp.float32),
        ],
        in_specs=[SMEM, SMEM, SMEM, VMEM],
        out_specs=[SMEM, VMEM, VMEM],
        compiler_params=pltpu.CompilerParams(vmem_limit_bytes=4 * 2**20),
        name="plan",
    )(screening, tile_slot, occ, virt)


def columns_of(bufs):
    return [(buf, n) for buf in bufs for n in range(buf.shape[0])]


def right_product(base, dims, table, amp, bufs, out):
    _, _, row_tiles, shifts, tile = dims
    sources = columns_of(bufs)
    half = len(sources) // 2
    zero = jnp.zeros((tile, tile), jnp.bfloat16)
    for m in range(0, len(sources), 2):
        pair, block = [], []
        for n in (m, m + 1):
            buf, k = sources[n]
            pair.append(buf[k])
            at = table[base + n % half + n // half * shifts]
            block.append(amp[:, pl.ds(pl.multiple_of(at * tile, tile), tile)])
        n_q = pair[0].shape[0]
        rhs = jnp.concatenate(
            [
                jnp.concatenate(((x[q], zero), (zero, x[q]))[j], axis=1)
                for q in range(n_q)
                for j, x in enumerate(pair)
            ],
            axis=0,
        )
        done = lax.dot_general(
            jnp.concatenate(block, axis=1),
            rhs,
            (((1,), (1,)), ((), ())),
            preferred_element_type=jnp.float32,
        ).astype(jnp.bfloat16)
        for i in range(row_tiles):
            for q in range(n_q):
                out[i, q, :, m * tile : (m + 2) * tile] = done[
                    i * tile : (i + 1) * tile, q * 2 * tile : (q + 1) * 2 * tile
                ]


def right_kernel(base, dims, table, amp, *refs):
    *bufs, out = refs
    right_product(base, dims, table, amp, bufs, out)


def product_shape(dims, bufs):
    _, _, row_tiles, shifts, tile = dims
    return (row_tiles, bufs[0].shape[1], tile, shifts * tile)


def right(base, dims, table, amp, bufs):
    shape = product_shape(dims, bufs)
    flops = 2 * amp.shape[0] * shape[1] * shape[3] * shape[2]
    return pl.pallas_call(
        functools.partial(right_kernel, base, dims),
        out_shape=jax.ShapeDtypeStruct(shape, jnp.bfloat16),
        in_specs=[SMEM] + [VMEM] * (1 + len(bufs)),
        out_specs=VMEM,
        compiler_params=pltpu.CompilerParams(vmem_limit_bytes=10 * 2**20),
        cost_estimate=pl.CostEstimate(flops=flops, bytes_accessed=0, transcendentals=0),
        name="right",
    )(table, amp, *bufs)


def left_kernel(dims, sizes, table, row_den, col_e, amp, *refs):
    _, _, row_tiles, shifts, tile = dims
    own, cross, refs = refs[:sizes], refs[sizes : 2 * sizes], refs[2 * sizes :]
    near_own, far_own, near_cross, out, far_cross, left, held, sems = refs
    half = shifts // 2
    n_q = own[0].shape[1]
    bounds = [0]
    for buf in own:
        bounds.append(bounds[-1] + buf.shape[0])
    for i in range(row_tiles):
        source = table[2 * shifts + i]
        shift, other = source % shifts, source // shifts
        rank = jnp.where(shift < half, 0, shifts) + other * half + shift % half
        for n in range(sizes):

            @pl.when((rank >= bounds[n]) & (rank < bounds[n + 1]))
            def _():
                for q in range(n_q):
                    left[i, :, q * tile : (q + 1) * tile] = own[n][rank - bounds[n], q]
                    at = (n_q + q) * tile
                    left[i, :, at : at + tile] = cross[n][rank - bounds[n], q]

    far = [buf for n, buf in enumerate(cross) if bounds[n] >= shifts]
    right_product(half, dims, table, amp, far, far_cross)
    writes = []
    for part, pieces in enumerate(((near_own, near_cross), (far_own, far_cross))):
        for m in range(0, shifts, 2):
            cols = slice(m * tile, (m + 2) * tile)
            ids = [part * half + n % half + n // half * shifts for n in (m, m + 1)]
            for i in range(row_tiles):
                rhs = jnp.concatenate(
                    [x[i, q, :, cols] for x in pieces for q in range(n_q)], axis=0
                )
                acc = jnp.dot(left[i], rhs, preferred_element_type=jnp.float32)
                for j, n in enumerate(ids):
                    den = row_den[i] + col_e[n : n + 1, :]
                    held[n, i * tile : (i + 1) * tile, :] = (
                        acc[:, j * tile : (j + 1) * tile] / den
                    )
            for n in ids:
                at = pl.ds(pl.multiple_of(table[n] * tile, tile), tile)
                copy = pltpu.make_async_copy(held.at[n], out.at[:, at], sems.at[n])
                copy.start()
                writes.append(copy)
    for copy in writes:
        copy.wait()


def left_product(dims, table, row_den, col_e, amp, own, cross, done):
    _, _, row_tiles, shifts, tile = dims
    rows, columns = amp.shape
    count, n_q = 2 * shifts, own[0].shape[1]
    return pl.pallas_call(
        functools.partial(left_kernel, dims, len(own)),
        out_shape=jax.ShapeDtypeStruct((rows, columns), jnp.float32),
        in_specs=[SMEM] + [VMEM] * (3 + 2 * len(own) + len(done)),
        out_specs=ANY,
        scratch_shapes=[
            pltpu.VMEM(product_shape(dims, own), jnp.bfloat16),
            pltpu.VMEM((row_tiles, tile, 2 * n_q * tile), jnp.bfloat16),
            pltpu.VMEM((count, rows, tile), jnp.float32),
            pltpu.SemaphoreType.DMA((count,)),
        ],
        compiler_params=pltpu.CompilerParams(vmem_limit_bytes=24 * 2**20),
        name="left",
    )(table, row_den, col_e, amp, *own, *cross, *done)


def crossings(shifts):
    half = shifts // 2
    early = [[s] for s in (0, 1, half, half + 1)]
    near = [[s, s + 1] for s in range(2, half, 2)]
    return early + near + [[s] for s in range(half + 2, shifts)]


def direct(
    amplitudes, factors, screening, tile_slot, pair_orbitals, occupied_energy, virtual_energy
):
    tile_dev, _, tile, _ = factors.shape
    n_pair, n_cut = lax.axis_size("pair"), lax.axis_size("cuts")
    group = n_pair // screening.shape[0]
    shifts = n_pair // group
    half = shifts // 2
    row_tiles = amplitudes.shape[0] // tile // n_cut
    me = lax.axis_index("pair")

    def send(x, move):
        pairs = [
            (p * n_cut + c, dst[0] * n_cut + dst[1])
            for p in range(n_pair)
            for c in range(n_cut)
            for dst in [move(p, c)]
        ]
        return lax.ppermute(x, BOTH, pairs)

    def over(x):
        return send(x, lambda p, c: (p ^ 1, c))

    picked = pick(screening, tile_slot, factors, group, shifts)
    got = [picked[0]] + [
        send(picked[s], lambda p, c: (p ^ (s * group), c))
        for s in range(1, shifts)
    ]
    crossed = [None] * shifts
    for members in crossings(shifts):
        x = got[members[0]]
        if len(members) > 1:
            x = jnp.stack([got[s] for s in members])
        x = send(x, lambda p, c: (p, c ^ 1))
        for n, s in enumerate(members):
            crossed[s] = x[n] if len(members) > 1 else x
    occ = occupied_energy[pair_orbitals[me // group]]
    rows = row_tiles * tile
    amp = lax.dynamic_slice_in_dim(amplitudes, lax.axis_index("cuts") * rows, rows, 0)
    dims = (tile_dev, group, row_tiles, shifts, tile)
    table, row_den, col_e = plan(screening, tile_slot, occ, virtual_energy, dims)
    quarter = half + half // 2
    sides, done = [], []
    for n, held in enumerate((got, crossed)):
        mine, other = [], []
        for lo, hi in ((0, half), (half, quarter), (quarter, shifts)):
            mine.append(jnp.stack(held[lo:hi]))
            other.append(over(mine[-1]))
        near, far = [mine[0], other[0]], mine[1:] + other[1:]
        sides.append(near + far)
        for m, (base, bufs) in enumerate(((0, near), (half, far))):
            if (n, m) != (1, 1):
                done.append(right(base, dims, table, amp, bufs))
    return left_product(dims, table, row_den, col_e, amp, *sides, done)


def general(
    amplitudes, factors, screening, tile_slot, pair_orbitals, occupied_energy, virtual_energy
):
    tile_dev, q_cut, tile, _ = factors.shape
    count = screening.shape[1]
    me = lax.axis_index("pair")
    row_tiles = amplitudes.shape[0] // tile
    first_tile = me * row_tiles
    pair_id, tile_start = first_tile // count, first_tile % count
    my_tiles = screening[pair_id]
    my_slots = tile_slot[my_tiles]
    device_pairs = jnp.arange(lax.axis_size("pair"), dtype=jnp.int32) * row_tiles // count
    slot_table = tile_slot[screening[device_pairs]]
    wanted = slot_table // tile_dev == me
    local = jnp.sum(jnp.where(wanted, slot_table % tile_dev, 0), axis=1)
    needed = jnp.any(wanted, axis=1)
    outgoing = jnp.where(
        needed[:, None, None, None], factors[local], jnp.zeros((), factors.dtype)
    )
    incoming = lax.all_to_all(outgoing, "pair", split_axis=0, concat_axis=0, tiled=True)
    chosen = incoming[my_slots // tile_dev]
    left = lax.dynamic_slice_in_dim(chosen, tile_start, row_tiles, 0)
    blocks = amplitudes.reshape(row_tiles, tile, count * tile)
    total = jnp.zeros((row_tiles, tile, count, tile), jnp.float32)
    for q in range(q_cut):
        half = jnp.einsum(
            "iac,icx->iax", left[:, q], blocks, preferred_element_type=jnp.float32
        )
        half = half.astype(jnp.bfloat16).reshape(row_tiles, tile, count, tile)
        total = total + jnp.einsum(
            "iajd,jbd->iajb", half, chosen[:, q], preferred_element_type=jnp.float32
        )
    partial = total.reshape(row_tiles * tile, count * tile).astype(jnp.bfloat16)
    summed = lax.psum_scatter(partial, "cuts", scatter_dimension=0, tiled=True)
    occ = occupied_energy[pair_orbitals[pair_id]]
    energy = virtual_energy[my_tiles].reshape(count * tile)
    rows = summed.shape[0]
    begin = tile_start * tile + lax.axis_index("cuts") * rows
    row_energy = lax.dynamic_slice_in_dim(energy - occ[0], begin, rows, 0)
    return summed.astype(jnp.float32) / (row_energy[:, None] + (energy - occ[1])[None, :])


def solution(mesh):
    n_pair, n_cut = mesh.shape["pair"], mesh.shape["cuts"]

    def build(body):
        return jax.shard_map(
            body,
            mesh=mesh,
            in_specs=(P("pair", None), P("pair", "cuts", None, None), P(), P(), P(), P(), P()),
            out_specs=P(BOTH, None),
            check_vma=False,
        )

    def whole(amplitudes, factors, screening, *rest):
        n_pos, count = screening.shape
        every_owner = count == n_pair and n_pair == 2 * n_pos and n_pos & (n_pos - 1) == 0
        if not (every_owner and n_cut == 2):
            return build(general)(amplitudes, factors, screening, *rest)
        step = build(direct)
        return step(amplitudes, factors, screening, *rest)

    return whole
```

```python
import functools

import jax
import jax.numpy as jnp
from jax import lax
from jax.experimental import pallas as pl
from jax.experimental.pallas import tpu as pltpu
from jax.sharding import PartitionSpec as P


BOTH = ("pair", "cuts")
ANY = pl.BlockSpec(memory_space=pl.ANY)
SMEM = pl.BlockSpec(memory_space=pltpu.SMEM)
VMEM = pl.BlockSpec(memory_space=pltpu.VMEM)


def pick_kernel(tile_dev, group, screening, tile_slot, factors, *refs):
    *outs, shown, slots, held, sems = refs
    copies = [
        pltpu.make_async_copy(screening, shown, sems.at[0]),
        pltpu.make_async_copy(tile_slot, slots, sems.at[1]),
        pltpu.make_async_copy(factors, held, sems.at[2]),
    ]
    for copy in copies:
        copy.start()
    me = lax.axis_index("pair")
    copies[1].wait()
    tiles = [jnp.int32(0)] * tile_dev
    for t in range(tile_slot.shape[0]):
        slot = slots[t]
        tiles = [jnp.where(slot == me * tile_dev + n, t, x) for n, x in enumerate(tiles)]
    copies[0].wait()
    local = []
    for shift in range(len(outs)):
        peer = (me // group) ^ shift
        found = jnp.int32(0)
        for t in range(screening.shape[1]):
            tile = shown[peer, t]
            for n in range(1, tile_dev):
                found = jnp.where(tile == tiles[n], n, found)
        local.append(found)
    copies[2].wait()
    copies = [
        pltpu.make_async_copy(held.at[found], out, sems.at[3 + n])
        for n, (out, found) in enumerate(zip(outs, local))
    ]
    for copy in copies:
        copy.start()
    for copy in copies:
        copy.wait()


def pick(screening, tile_slot, factors, group, shifts):
    tile_dev, *tail = factors.shape
    hbm = pl.BlockSpec(memory_space=pltpu.HBM)
    return pl.pallas_call(
        functools.partial(pick_kernel, tile_dev, group),
        out_shape=[jax.ShapeDtypeStruct(tail, factors.dtype)] * shifts,
        in_specs=[hbm, hbm, hbm],
        out_specs=[ANY] * shifts,
        scratch_shapes=[
            pltpu.SMEM(screening.shape, jnp.int32),
            pltpu.SMEM(tile_slot.shape, jnp.int32),
            pltpu.VMEM(factors.shape, factors.dtype),
            pltpu.SemaphoreType.DMA((3 + shifts,)),
        ],
        name="pick",
    )(screening, tile_slot, factors)


def plan_kernel(dims, screening, tile_slot, orbitals, occupied, virtual, *refs):
    tile_dev, group, row_tiles, shifts, tile = dims
    table, row_den, col_e, *held, sems = refs
    given = (screening, tile_slot, orbitals, occupied, virtual)
    copies = [
        pltpu.make_async_copy(x, y, sems.at[n]) for n, (x, y) in enumerate(zip(given, held))
    ]
    for copy in copies:
        copy.start()
    for copy in copies:
        copy.wait()
    screening, tile_slot, orbitals, occupied, virt = held
    me, cut = lax.axis_index("pair"), lax.axis_index("cuts")
    pair_id, core = me // group, me % group
    count = screening.shape[1]
    first = core * (count // group) + cut * row_tiles
    occ = [occupied[orbitals[n, pair_id]] for n in range(2)]

    def source(t):
        slot = tile_slot[screening[pair_id, t]]
        owner = slot // tile_dev
        shift = (owner // group) ^ pair_id
        return shift + (owner % group ^ core) * shifts

    for t in range(count):
        n = source(t)
        table[n] = t
        col_e[pl.ds(n, 1), :] = virt[pl.ds(screening[pair_id, t], 1), :] - occ[1]
    for i in range(row_tiles):
        table[count + i] = source(first + i)
        row = virt[pl.ds(screening[pair_id, first + i], 1), :] - occ[0]
        row_den[i] = jnp.broadcast_to(row, (tile, tile)).T


def plan(screening, tile_slot, orbitals, occupied, virtual, dims):
    _, _, row_tiles, _, tile = dims
    count = screening.shape[1]
    return pl.pallas_call(
        functools.partial(plan_kernel, dims),
        out_shape=[
            jax.ShapeDtypeStruct((count + row_tiles,), jnp.int32),
            jax.ShapeDtypeStruct((row_tiles, tile, tile), jnp.float32),
            jax.ShapeDtypeStruct((count, tile), jnp.float32),
        ],
        in_specs=[pl.BlockSpec(memory_space=pltpu.HBM)] * 5,
        out_specs=[SMEM, VMEM, VMEM],
        scratch_shapes=[
            pltpu.SMEM(screening.shape, jnp.int32),
            pltpu.SMEM(tile_slot.shape, jnp.int32),
            pltpu.SMEM(orbitals.shape, jnp.int32),
            pltpu.SMEM(occupied.shape, jnp.float32),
            pltpu.VMEM(virtual.shape, jnp.float32),
            pltpu.SemaphoreType.DMA((5,)),
        ],
        name="plan",
    )(screening, tile_slot, orbitals, occupied, virtual)


def columns_of(bufs):
    return [(buf, n) for buf in bufs for n in range(buf.shape[0])]


def right_product(base, dims, table, amp, bufs, out):
    _, _, row_tiles, shifts, tile = dims
    sources = columns_of(bufs)
    half = len(sources) // 2
    zero = jnp.zeros((tile, tile), jnp.bfloat16)
    for m in range(0, len(sources), 2):
        pair, block = [], []
        for n in (m, m + 1):
            buf, k = sources[n]
            pair.append(buf[k])
            at = table[base + n % half + n // half * shifts]
            block.append(amp[:, pl.ds(pl.multiple_of(at * tile, tile), tile)])
        n_q = pair[0].shape[0]
        rhs = jnp.concatenate(
            [
                jnp.concatenate(((x[q], zero), (zero, x[q]))[j], axis=1)
                for q in range(n_q)
                for j, x in enumerate(pair)
            ],
            axis=0,
        )
        done = lax.dot_general(
            jnp.concatenate(block, axis=1),
            rhs,
            (((1,), (1,)), ((), ())),
            preferred_element_type=jnp.float32,
        ).astype(jnp.bfloat16)
        for i in range(row_tiles):
            for q in range(n_q):
                out[i, q, :, m * tile : (m + 2) * tile] = done[
                    i * tile : (i + 1) * tile, q * 2 * tile : (q + 1) * 2 * tile
                ]


def right_kernel(base, dims, table, amp, *refs):
    *bufs, out = refs
    right_product(base, dims, table, amp, bufs, out)


def product_shape(dims, bufs):
    _, _, row_tiles, shifts, tile = dims
    return (row_tiles, bufs[0].shape[1], tile, shifts * tile)


def right(base, dims, table, amp, bufs):
    shape = product_shape(dims, bufs)
    flops = 2 * amp.shape[0] * shape[1] * shape[3] * shape[2]
    return pl.pallas_call(
        functools.partial(right_kernel, base, dims),
        out_shape=jax.ShapeDtypeStruct(shape, jnp.bfloat16),
        in_specs=[SMEM] + [VMEM] * (1 + len(bufs)),
        out_specs=VMEM,
        compiler_params=pltpu.CompilerParams(vmem_limit_bytes=10 * 2**20),
        cost_estimate=pl.CostEstimate(flops=flops, bytes_accessed=0, transcendentals=0),
        name="right",
    )(table, amp, *bufs)


def left_kernel(dims, sizes, table, row_den, col_e, amp, *refs):
    _, _, row_tiles, shifts, tile = dims
    own, cross, refs = refs[:sizes], refs[sizes : 2 * sizes], refs[2 * sizes :]
    near_own, far_own, near_cross, out, far_cross, left, held, sems = refs
    half = shifts // 2
    n_q = own[0].shape[1]
    bounds = [0]
    for buf in own:
        bounds.append(bounds[-1] + buf.shape[0])
    for i in range(row_tiles):
        source = table[2 * shifts + i]
        shift, other = source % shifts, source // shifts
        rank = jnp.where(shift < half, 0, shifts) + other * half + shift % half
        for n in range(sizes):

            @pl.when((rank >= bounds[n]) & (rank < bounds[n + 1]))
            def _():
                for q in range(n_q):
                    left[i, :, q * tile : (q + 1) * tile] = own[n][rank - bounds[n], q]
                    at = (n_q + q) * tile
                    left[i, :, at : at + tile] = cross[n][rank - bounds[n], q]

    far = [buf for n, buf in enumerate(cross) if bounds[n] >= shifts]
    right_product(half, dims, table, amp, far, far_cross)
    writes = []
    for part, pieces in enumerate(((near_own, near_cross), (far_own, far_cross))):
        for m in range(0, shifts, 2):
            cols = slice(m * tile, (m + 2) * tile)
            ids = [part * half + n % half + n // half * shifts for n in (m, m + 1)]
            for i in range(row_tiles):
                rhs = jnp.concatenate(
                    [x[i, q, :, cols] for x in pieces for q in range(n_q)], axis=0
                )
                acc = jnp.dot(left[i], rhs, preferred_element_type=jnp.float32)
                for j, n in enumerate(ids):
                    den = row_den[i] + col_e[n : n + 1, :]
                    held[n, i * tile : (i + 1) * tile, :] = (
                        acc[:, j * tile : (j + 1) * tile] / den
                    )
            for n in ids:
                at = pl.ds(pl.multiple_of(table[n] * tile, tile), tile)
                copy = pltpu.make_async_copy(held.at[n], out.at[:, at], sems.at[n])
                copy.start()
                writes.append(copy)
    for copy in writes:
        copy.wait()


def left_product(dims, table, row_den, col_e, amp, own, cross, done):
    _, _, row_tiles, shifts, tile = dims
    rows, columns = amp.shape
    count, n_q = 2 * shifts, own[0].shape[1]
    return pl.pallas_call(
        functools.partial(left_kernel, dims, len(own)),
        out_shape=jax.ShapeDtypeStruct((rows, columns), jnp.float32),
        in_specs=[SMEM] + [VMEM] * (3 + 2 * len(own) + len(done)),
        out_specs=ANY,
        scratch_shapes=[
            pltpu.VMEM(product_shape(dims, own), jnp.bfloat16),
            pltpu.VMEM((row_tiles, tile, 2 * n_q * tile), jnp.bfloat16),
            pltpu.VMEM((count, rows, tile), jnp.float32),
            pltpu.SemaphoreType.DMA((count,)),
        ],
        compiler_params=pltpu.CompilerParams(vmem_limit_bytes=24 * 2**20),
        name="left",
    )(table, row_den, col_e, amp, *own, *cross, *done)


def crossings(shifts):
    half = shifts // 2
    early = [[s] for s in (0, 1, half, half + 1)]
    near = [[s, s + 1] for s in range(2, half, 2)]
    return early + near + [[s] for s in range(half + 2, shifts)]


def direct(
    amplitudes, factors, screening, tile_slot, pair_orbitals, occupied_energy, virtual_energy
):
    tile_dev, _, tile, _ = factors.shape
    n_pair, n_cut = lax.axis_size("pair"), lax.axis_size("cuts")
    group = n_pair // screening.shape[0]
    shifts = n_pair // group
    half = shifts // 2
    row_tiles = amplitudes.shape[0] // tile // n_cut

    def send(x, move):
        pairs = [
            (p * n_cut + c, dst[0] * n_cut + dst[1])
            for p in range(n_pair)
            for c in range(n_cut)
            for dst in [move(p, c)]
        ]
        return lax.ppermute(x, BOTH, pairs)

    def over(x):
        return send(x, lambda p, c: (p ^ 1, c))

    picked = pick(screening, tile_slot, factors, group, shifts)
    got = [picked[0]] + [
        send(picked[s], lambda p, c: (p ^ (s * group), c))
        for s in range(1, shifts)
    ]
    crossed = [None] * shifts
    for members in crossings(shifts):
        x = got[members[0]]
        if len(members) > 1:
            x = jnp.stack([got[s] for s in members])
        x = send(x, lambda p, c: (p, c ^ 1))
        for n, s in enumerate(members):
            crossed[s] = x[n] if len(members) > 1 else x
    rows = row_tiles * tile
    amp = lax.dynamic_slice_in_dim(amplitudes, lax.axis_index("cuts") * rows, rows, 0)
    dims = (tile_dev, group, row_tiles, shifts, tile)
    table, row_den, col_e = plan(
        screening, tile_slot, pair_orbitals.T, occupied_energy, virtual_energy, dims
    )
    quarter = half + half // 2
    sides, done = [], []
    for n, held in enumerate((got, crossed)):
        mine, other = [], []
        for lo, hi in ((0, half), (half, quarter), (quarter, shifts)):
            mine.append(jnp.stack(held[lo:hi]))
            other.append(over(mine[-1]))
        near, far = [mine[0], other[0]], mine[1:] + other[1:]
        sides.append(near + far)
        for m, (base, bufs) in enumerate(((0, near), (half, far))):
            if (n, m) != (1, 1):
                done.append(right(base, dims, table, amp, bufs))
    return left_product(dims, table, row_den, col_e, amp, *sides, done)


def general(
    amplitudes, factors, screening, tile_slot, pair_orbitals, occupied_energy, virtual_energy
):
    tile_dev, q_cut, tile, _ = factors.shape
    count = screening.shape[1]
    me = lax.axis_index("pair")
    row_tiles = amplitudes.shape[0] // tile
    first_tile = me * row_tiles
    pair_id, tile_start = first_tile // count, first_tile % count
    my_tiles = screening[pair_id]
    my_slots = tile_slot[my_tiles]
    device_pairs = jnp.arange(lax.axis_size("pair"), dtype=jnp.int32) * row_tiles // count
    slot_table = tile_slot[screening[device_pairs]]
    wanted = slot_table // tile_dev == me
    local = jnp.sum(jnp.where(wanted, slot_table % tile_dev, 0), axis=1)
    needed = jnp.any(wanted, axis=1)
    outgoing = jnp.where(
        needed[:, None, None, None], factors[local], jnp.zeros((), factors.dtype)
    )
    incoming = lax.all_to_all(outgoing, "pair", split_axis=0, concat_axis=0, tiled=True)
    chosen = incoming[my_slots // tile_dev]
    left = lax.dynamic_slice_in_dim(chosen, tile_start, row_tiles, 0)
    blocks = amplitudes.reshape(row_tiles, tile, count * tile)
    total = jnp.zeros((row_tiles, tile, count, tile), jnp.float32)
    for q in range(q_cut):
        half = jnp.einsum(
            "iac,icx->iax", left[:, q], blocks, preferred_element_type=jnp.float32
        )
        half = half.astype(jnp.bfloat16).reshape(row_tiles, tile, count, tile)
        total = total + jnp.einsum(
            "iajd,jbd->iajb", half, chosen[:, q], preferred_element_type=jnp.float32
        )
    partial = total.reshape(row_tiles * tile, count * tile).astype(jnp.bfloat16)
    summed = lax.psum_scatter(partial, "cuts", scatter_dimension=0, tiled=True)
    occ = occupied_energy[pair_orbitals[pair_id]]
    energy = virtual_energy[my_tiles].reshape(count * tile)
    rows = summed.shape[0]
    begin = tile_start * tile + lax.axis_index("cuts") * rows
    row_energy = lax.dynamic_slice_in_dim(energy - occ[0], begin, rows, 0)
    return summed.astype(jnp.float32) / (row_energy[:, None] + (energy - occ[1])[None, :])


def solution(mesh):
    n_pair, n_cut = mesh.shape["pair"], mesh.shape["cuts"]

    def build(body):
        return jax.shard_map(
            body,
            mesh=mesh,
            in_specs=(P("pair", None), P("pair", "cuts", None, None), P(), P(), P(), P(), P()),
            out_specs=P(BOTH, None),
            check_vma=False,
        )

    def whole(amplitudes, factors, screening, *rest):
        n_pos, count = screening.shape
        every_owner = count == n_pair and n_pair == 2 * n_pos and n_pos & (n_pos - 1) == 0
        if not (every_owner and n_cut == 2):
            return build(general)(amplitudes, factors, screening, *rest)
        step = build(direct)
        return step(amplitudes, factors, screening, *rest)

    return whole
```

```python
import functools

import jax
import jax.numpy as jnp
from jax import lax
from jax.experimental import pallas as pl
from jax.experimental.pallas import tpu as pltpu
from jax.sharding import PartitionSpec as P


BOTH = ("pair", "cuts")
ANY = pl.BlockSpec(memory_space=pl.ANY)
SMEM = pl.BlockSpec(memory_space=pltpu.SMEM)
VMEM = pl.BlockSpec(memory_space=pltpu.VMEM)


def pick_kernel(tile_dev, group, screening, tile_slot, factors, *refs):
    *outs, shown, slots, held, sems = refs
    copies = [
        pltpu.make_async_copy(screening, shown, sems.at[0]),
        pltpu.make_async_copy(tile_slot, slots, sems.at[1]),
        pltpu.make_async_copy(factors, held, sems.at[2]),
    ]
    for copy in copies:
        copy.start()
    me = lax.axis_index("pair")
    copies[1].wait()
    tiles = [jnp.int32(0)] * tile_dev
    for t in range(tile_slot.shape[0]):
        slot = slots[t]
        tiles = [jnp.where(slot == me * tile_dev + n, t, x) for n, x in enumerate(tiles)]
    copies[0].wait()
    local = []
    for shift in range(len(outs)):
        peer = (me // group) ^ shift
        found = jnp.int32(0)
        for t in range(screening.shape[1]):
            tile = shown[peer, t]
            for n in range(1, tile_dev):
                found = jnp.where(tile == tiles[n], n, found)
        local.append(found)
    copies[2].wait()
    copies = [
        pltpu.make_async_copy(held.at[found], out, sems.at[3 + n])
        for n, (out, found) in enumerate(zip(outs, local))
    ]
    for copy in copies:
        copy.start()
    for copy in copies:
        copy.wait()


def pick(screening, tile_slot, factors, group, shifts):
    tile_dev, *tail = factors.shape
    hbm = pl.BlockSpec(memory_space=pltpu.HBM)
    return pl.pallas_call(
        functools.partial(pick_kernel, tile_dev, group),
        out_shape=[jax.ShapeDtypeStruct(tail, factors.dtype)] * shifts,
        in_specs=[hbm, hbm, hbm],
        out_specs=[ANY] * shifts,
        scratch_shapes=[
            pltpu.SMEM(screening.shape, jnp.int32),
            pltpu.SMEM(tile_slot.shape, jnp.int32),
            pltpu.VMEM(factors.shape, factors.dtype),
            pltpu.SemaphoreType.DMA((3 + shifts,)),
        ],
        name="pick",
    )(screening, tile_slot, factors)


def plan_kernel(dims, screening, tile_slot, orbitals, occupied, virtual, *refs):
    tile_dev, group, row_tiles, shifts, tile = dims
    table, row_den, col_e, *held, sems = refs
    given = (screening, tile_slot, orbitals, occupied, virtual)
    copies = [
        pltpu.make_async_copy(x, y, sems.at[n]) for n, (x, y) in enumerate(zip(given, held))
    ]
    for copy in copies:
        copy.start()
    for copy in copies:
        copy.wait()
    screening, tile_slot, orbitals, occupied, virt = held
    me, cut = lax.axis_index("pair"), lax.axis_index("cuts")
    pair_id, core = me // group, me % group
    count = screening.shape[1]
    first = core * (count // group) + cut * row_tiles
    occ = [occupied[orbitals[n, pair_id]] for n in range(2)]

    def source(t):
        slot = tile_slot[screening[pair_id, t]]
        owner = slot // tile_dev
        shift = (owner // group) ^ pair_id
        return shift + (owner % group ^ core) * shifts

    for t in range(count):
        n = source(t)
        table[n] = t
        col_e[pl.ds(n, 1), :] = virt[pl.ds(screening[pair_id, t], 1), :] - occ[1]
    for i in range(row_tiles):
        table[count + i] = source(first + i)
        row = virt[pl.ds(screening[pair_id, first + i], 1), :] - occ[0]
        row_den[i] = jnp.broadcast_to(row, (tile, tile)).T


def plan(screening, tile_slot, orbitals, occupied, virtual, dims):
    _, _, row_tiles, _, tile = dims
    count = screening.shape[1]
    return pl.pallas_call(
        functools.partial(plan_kernel, dims),
        out_shape=[
            jax.ShapeDtypeStruct((count + row_tiles,), jnp.int32),
            jax.ShapeDtypeStruct((row_tiles, tile, tile), jnp.float32),
            jax.ShapeDtypeStruct((count, tile), jnp.float32),
        ],
        in_specs=[pl.BlockSpec(memory_space=pltpu.HBM)] * 5,
        out_specs=[SMEM, VMEM, VMEM],
        scratch_shapes=[
            pltpu.SMEM(screening.shape, jnp.int32),
            pltpu.SMEM(tile_slot.shape, jnp.int32),
            pltpu.SMEM(orbitals.shape, jnp.int32),
            pltpu.SMEM(occupied.shape, jnp.float32),
            pltpu.VMEM(virtual.shape, jnp.float32),
            pltpu.SemaphoreType.DMA((5,)),
        ],
        name="plan",
    )(screening, tile_slot, orbitals, occupied, virtual)


def columns_of(bufs):
    return [(buf, n) for buf in bufs for n in range(buf.shape[0])]


def right_product(base, dims, table, amp, bufs, out):
    _, _, row_tiles, shifts, tile = dims
    sources = columns_of(bufs)
    half = len(sources) // 2
    zero = jnp.zeros((tile, tile), jnp.bfloat16)
    for m in range(0, len(sources), 2):
        pair, block = [], []
        for n in (m, m + 1):
            buf, k = sources[n]
            pair.append(buf[k])
            at = table[base + n % half + n // half * shifts]
            block.append(amp[:, pl.ds(pl.multiple_of(at * tile, tile), tile)])
        n_q = pair[0].shape[0]
        rhs = jnp.concatenate(
            [
                jnp.concatenate(((x[q], zero), (zero, x[q]))[j], axis=1)
                for q in range(n_q)
                for j, x in enumerate(pair)
            ],
            axis=0,
        )
        done = lax.dot_general(
            jnp.concatenate(block, axis=1),
            rhs,
            (((1,), (1,)), ((), ())),
            preferred_element_type=jnp.float32,
        ).astype(jnp.bfloat16)
        for i in range(row_tiles):
            for q in range(n_q):
                out[i, q, :, m * tile : (m + 2) * tile] = done[
                    i * tile : (i + 1) * tile, q * 2 * tile : (q + 1) * 2 * tile
                ]


def right_kernel(base, dims, table, amp, *refs):
    *bufs, out = refs
    right_product(base, dims, table, amp, bufs, out)


def product_shape(dims, bufs):
    _, _, row_tiles, shifts, tile = dims
    return (row_tiles, bufs[0].shape[1], tile, shifts * tile)


def right(base, dims, table, amp, bufs):
    shape = product_shape(dims, bufs)
    flops = 2 * amp.shape[0] * shape[1] * shape[3] * shape[2]
    return pl.pallas_call(
        functools.partial(right_kernel, base, dims),
        out_shape=jax.ShapeDtypeStruct(shape, jnp.bfloat16),
        in_specs=[SMEM] + [VMEM] * (1 + len(bufs)),
        out_specs=VMEM,
        compiler_params=pltpu.CompilerParams(vmem_limit_bytes=10 * 2**20),
        cost_estimate=pl.CostEstimate(flops=flops, bytes_accessed=0, transcendentals=0),
        name="right",
    )(table, amp, *bufs)


def left_kernel(dims, sizes, table, row_den, col_e, amp, *refs):
    _, _, row_tiles, shifts, tile = dims
    own, cross, refs = refs[:sizes], refs[sizes : 2 * sizes], refs[2 * sizes :]
    near_own, far_own, near_cross, out, far_cross, left, held, sems = refs
    half = shifts // 2
    n_q = own[0].shape[1]
    bounds = [0]
    for buf in own:
        bounds.append(bounds[-1] + buf.shape[0])
    for i in range(row_tiles):
        source = table[2 * shifts + i]
        shift, other = source % shifts, source // shifts
        rank = jnp.where(shift < half, 0, shifts) + other * half + shift % half
        for n in range(sizes):

            @pl.when((rank >= bounds[n]) & (rank < bounds[n + 1]))
            def _():
                for q in range(n_q):
                    left[i, :, q * tile : (q + 1) * tile] = own[n][rank - bounds[n], q]
                    at = (n_q + q) * tile
                    left[i, :, at : at + tile] = cross[n][rank - bounds[n], q]

    far = [buf for n, buf in enumerate(cross) if bounds[n] >= shifts]
    right_product(half, dims, table, amp, far, far_cross)
    writes = []
    for part, pieces in enumerate(((near_own, near_cross), (far_own, far_cross))):
        for m in range(0, shifts, 2):
            cols = slice(m * tile, (m + 2) * tile)
            ids = [part * half + n % half + n // half * shifts for n in (m, m + 1)]
            for i in range(row_tiles):
                rhs = jnp.concatenate(
                    [x[i, q, :, cols] for x in pieces for q in range(n_q)], axis=0
                )
                acc = jnp.dot(left[i], rhs, preferred_element_type=jnp.float32)
                for j, n in enumerate(ids):
                    den = row_den[i] + col_e[n : n + 1, :]
                    held[n, i * tile : (i + 1) * tile, :] = (
                        acc[:, j * tile : (j + 1) * tile] / den
                    )
            for n in ids:
                at = pl.ds(pl.multiple_of(table[n] * tile, tile), tile)
                copy = pltpu.make_async_copy(held.at[n], out.at[:, at], sems.at[n])
                copy.start()
                writes.append(copy)
    for copy in writes:
        copy.wait()


def left_product(dims, table, row_den, col_e, amp, own, cross, done):
    _, _, row_tiles, shifts, tile = dims
    rows, columns = amp.shape
    count, n_q = 2 * shifts, own[0].shape[1]
    return pl.pallas_call(
        functools.partial(left_kernel, dims, len(own)),
        out_shape=jax.ShapeDtypeStruct((rows, columns), jnp.float32),
        in_specs=[SMEM] + [VMEM] * (3 + 2 * len(own) + len(done)),
        out_specs=ANY,
        scratch_shapes=[
            pltpu.VMEM(product_shape(dims, own), jnp.bfloat16),
            pltpu.VMEM((row_tiles, tile, 2 * n_q * tile), jnp.bfloat16),
            pltpu.VMEM((count, rows, tile), jnp.float32),
            pltpu.SemaphoreType.DMA((count,)),
        ],
        compiler_params=pltpu.CompilerParams(vmem_limit_bytes=24 * 2**20),
        name="left",
    )(table, row_den, col_e, amp, *own, *cross, *done)


def direct(
    amplitudes, factors, screening, tile_slot, pair_orbitals, occupied_energy, virtual_energy
):
    tile_dev, _, tile, _ = factors.shape
    n_pair, n_cut = lax.axis_size("pair"), lax.axis_size("cuts")
    group = n_pair // screening.shape[0]
    shifts = n_pair // group
    half = shifts // 2
    row_tiles = amplitudes.shape[0] // tile // n_cut

    def send(x, move):
        pairs = [
            (p * n_cut + c, dst[0] * n_cut + dst[1])
            for p in range(n_pair)
            for c in range(n_cut)
            for dst in [move(p, c)]
        ]
        return lax.ppermute(x, BOTH, pairs)

    def over(x):
        return send(x, lambda p, c: (p ^ 1, c))

    picked = pick(screening, tile_slot, factors, group, shifts)
    got = [picked[0]] + [
        send(picked[s], lambda p, c: (p ^ (s * group), c))
        for s in range(1, shifts)
    ]
    crossed = [send(got[s], lambda p, c: (p, c ^ 1)) for s in range(shifts)]
    rows = row_tiles * tile
    amp = lax.dynamic_slice_in_dim(amplitudes, lax.axis_index("cuts") * rows, rows, 0)
    dims = (tile_dev, group, row_tiles, shifts, tile)
    table, row_den, col_e = plan(
        screening, tile_slot, pair_orbitals.T, occupied_energy, virtual_energy, dims
    )
    quarter = half + half // 2
    sides, done = [], []
    for n, held in enumerate((got, crossed)):
        mine, other = [], []
        for lo, hi in ((0, half), (half, quarter), (quarter, shifts)):
            mine.append(jnp.stack(held[lo:hi]))
            other.append(over(mine[-1]))
        near, far = [mine[0], other[0]], mine[1:] + other[1:]
        sides.append(near + far)
        for m, (base, bufs) in enumerate(((0, near), (half, far))):
            if (n, m) != (1, 1):
                done.append(right(base, dims, table, amp, bufs))
    return left_product(dims, table, row_den, col_e, amp, *sides, done)


def general(
    amplitudes, factors, screening, tile_slot, pair_orbitals, occupied_energy, virtual_energy
):
    tile_dev, q_cut, tile, _ = factors.shape
    count = screening.shape[1]
    me = lax.axis_index("pair")
    row_tiles = amplitudes.shape[0] // tile
    first_tile = me * row_tiles
    pair_id, tile_start = first_tile // count, first_tile % count
    my_tiles = screening[pair_id]
    my_slots = tile_slot[my_tiles]
    device_pairs = jnp.arange(lax.axis_size("pair"), dtype=jnp.int32) * row_tiles // count
    slot_table = tile_slot[screening[device_pairs]]
    wanted = slot_table // tile_dev == me
    local = jnp.sum(jnp.where(wanted, slot_table % tile_dev, 0), axis=1)
    needed = jnp.any(wanted, axis=1)
    outgoing = jnp.where(
        needed[:, None, None, None], factors[local], jnp.zeros((), factors.dtype)
    )
    incoming = lax.all_to_all(outgoing, "pair", split_axis=0, concat_axis=0, tiled=True)
    chosen = incoming[my_slots // tile_dev]
    left = lax.dynamic_slice_in_dim(chosen, tile_start, row_tiles, 0)
    blocks = amplitudes.reshape(row_tiles, tile, count * tile)
    total = jnp.zeros((row_tiles, tile, count, tile), jnp.float32)
    for q in range(q_cut):
        half = jnp.einsum(
            "iac,icx->iax", left[:, q], blocks, preferred_element_type=jnp.float32
        )
        half = half.astype(jnp.bfloat16).reshape(row_tiles, tile, count, tile)
        total = total + jnp.einsum(
            "iajd,jbd->iajb", half, chosen[:, q], preferred_element_type=jnp.float32
        )
    partial = total.reshape(row_tiles * tile, count * tile).astype(jnp.bfloat16)
    summed = lax.psum_scatter(partial, "cuts", scatter_dimension=0, tiled=True)
    occ = occupied_energy[pair_orbitals[pair_id]]
    energy = virtual_energy[my_tiles].reshape(count * tile)
    rows = summed.shape[0]
    begin = tile_start * tile + lax.axis_index("cuts") * rows
    row_energy = lax.dynamic_slice_in_dim(energy - occ[0], begin, rows, 0)
    return summed.astype(jnp.float32) / (row_energy[:, None] + (energy - occ[1])[None, :])


def solution(mesh):
    n_pair, n_cut = mesh.shape["pair"], mesh.shape["cuts"]

    def build(body):
        return jax.shard_map(
            body,
            mesh=mesh,
            in_specs=(P("pair", None), P("pair", "cuts", None, None), P(), P(), P(), P(), P()),
            out_specs=P(BOTH, None),
            check_vma=False,
        )

    def whole(amplitudes, factors, screening, *rest):
        n_pos, count = screening.shape
        every_owner = count == n_pair and n_pair == 2 * n_pos and n_pos & (n_pos - 1) == 0
        if not (every_owner and n_cut == 2):
            return build(general)(amplitudes, factors, screening, *rest)
        step = build(direct)
        return step(amplitudes, factors, screening, *rest)

    return whole
```

```python
import functools

import jax
import jax.numpy as jnp
from jax import lax
from jax.experimental import pallas as pl
from jax.experimental.pallas import tpu as pltpu
from jax.sharding import PartitionSpec as P


BOTH = ("pair", "cuts")
ANY = pl.BlockSpec(memory_space=pl.ANY)
SMEM = pl.BlockSpec(memory_space=pltpu.SMEM)
VMEM = pl.BlockSpec(memory_space=pltpu.VMEM)


def pick_kernel(dims, *refs):
    tile_dev, group, row_tiles, shifts, _ = dims
    given, outs, held = refs[:6], refs[6 : 8 + shifts], refs[8 + shifts :]
    *held, table, energy, sems, done = held
    fetch = [pltpu.make_async_copy(x, y, sems.at[n]) for n, (x, y) in enumerate(zip(given, held))]
    for copy in fetch:
        copy.start()
    screening, tile_slot, factors, orbitals, occupied, virt = held
    me, cut = lax.axis_index("pair"), lax.axis_index("cuts")
    pair_id, core = me // group, me % group
    count = screening.shape[1]
    fetch[1].wait()
    tiles = [jnp.int32(0)] * tile_dev
    for t in range(tile_slot.shape[0]):
        slot = tile_slot[t]
        tiles = [jnp.where(slot == me * tile_dev + n, t, x) for n, x in enumerate(tiles)]
    fetch[0].wait()
    local = []
    for shift in range(shifts):
        found = jnp.int32(0)
        for t in range(count):
            for n in range(1, tile_dev):
                found = jnp.where(screening[pair_id ^ shift, t] == tiles[n], n, found)
        local.append(found)
    fetch[2].wait()
    sent = []
    for shift, found in enumerate(local):
        sent.append(pltpu.make_async_copy(factors.at[found], outs[shift], done.at[shift]))
        sent[-1].start()
    for copy in fetch[3:]:
        copy.wait()
    first = core * (count // group) + cut * row_tiles
    occ = [occupied[orbitals[n, pair_id]] for n in range(2)]

    def source(t):
        slot = tile_slot[screening[pair_id, t]]
        owner = slot // tile_dev
        shift = (owner // group) ^ pair_id
        return shift + (owner % group ^ core) * shifts

    for t in range(count):
        n = source(t)
        table[n] = t
        energy[pl.ds(n, 1), :] = virt[pl.ds(screening[pair_id, t], 1), :] - occ[1]
    for i in range(row_tiles):
        table[count + i] = source(first + i)
        energy[count + i : count + i + 1, :] = (
            virt[pl.ds(screening[pair_id, first + i], 1), :] - occ[0]
        )
    for n, x in enumerate((table, energy)):
        sent.append(pltpu.make_async_copy(x, outs[shifts + n], done.at[shifts + n]))
        sent[-1].start()
    for copy in sent:
        copy.wait()


def pick(dims, screening, tile_slot, factors, orbitals, occupied, virtual):
    _, _, row_tiles, shifts, tile = dims
    lines = screening.shape[1] + row_tiles
    return pl.pallas_call(
        functools.partial(pick_kernel, dims),
        out_shape=[jax.ShapeDtypeStruct(factors.shape[1:], factors.dtype)] * shifts
        + [
            jax.ShapeDtypeStruct((lines,), jnp.int32),
            jax.ShapeDtypeStruct((lines, tile), jnp.float32),
        ],
        in_specs=[ANY] * 6,
        out_specs=[ANY] * (shifts + 2),
        scratch_shapes=[
            pltpu.SMEM(screening.shape, jnp.int32),
            pltpu.SMEM(tile_slot.shape, jnp.int32),
            pltpu.VMEM(factors.shape, factors.dtype),
            pltpu.SMEM(orbitals.shape, jnp.int32),
            pltpu.SMEM(occupied.shape, jnp.float32),
            pltpu.VMEM(virtual.shape, jnp.float32),
            pltpu.SMEM((lines,), jnp.int32),
            pltpu.VMEM((lines, tile), jnp.float32),
            pltpu.SemaphoreType.DMA((6,)),
            pltpu.SemaphoreType.DMA((shifts + 2,)),
        ],
        name="pick",
    )(screening, tile_slot, factors, orbitals, occupied, virtual)


def columns_of(bufs):
    return [(buf, n) for buf in bufs for n in range(buf.shape[0])]


def right_product(base, dims, table, amp, bufs, out):
    _, _, row_tiles, shifts, tile = dims
    sources = columns_of(bufs)
    half = len(sources) // 2
    zero = jnp.zeros((tile, tile), jnp.bfloat16)
    for m in range(0, len(sources), 2):
        pair, block = [], []
        for n in (m, m + 1):
            buf, k = sources[n]
            pair.append(buf[k])
            at = table[base + n % half + n // half * shifts]
            block.append(amp[:, pl.ds(pl.multiple_of(at * tile, tile), tile)])
        n_q = pair[0].shape[0]
        rhs = jnp.concatenate(
            [
                jnp.concatenate(((x[q], zero), (zero, x[q]))[j], axis=1)
                for q in range(n_q)
                for j, x in enumerate(pair)
            ],
            axis=0,
        )
        done = lax.dot_general(
            jnp.concatenate(block, axis=1),
            rhs,
            (((1,), (1,)), ((), ())),
            preferred_element_type=jnp.float32,
        ).astype(jnp.bfloat16)
        for i in range(row_tiles):
            for q in range(n_q):
                out[i, q, :, m * tile : (m + 2) * tile] = done[
                    i * tile : (i + 1) * tile, q * 2 * tile : (q + 1) * 2 * tile
                ]


def right_kernel(base, dims, table, amp, *refs):
    *bufs, out = refs
    right_product(base, dims, table, amp, bufs, out)


def product_shape(dims, bufs):
    _, _, row_tiles, shifts, tile = dims
    return (row_tiles, bufs[0].shape[1], tile, shifts * tile)


def right(base, dims, table, amp, bufs):
    shape = product_shape(dims, bufs)
    flops = 2 * amp.shape[0] * shape[1] * shape[3] * shape[2]
    return pl.pallas_call(
        functools.partial(right_kernel, base, dims),
        out_shape=jax.ShapeDtypeStruct(shape, jnp.bfloat16),
        in_specs=[SMEM] + [VMEM] * (1 + len(bufs)),
        out_specs=VMEM,
        compiler_params=pltpu.CompilerParams(vmem_limit_bytes=10 * 2**20),
        cost_estimate=pl.CostEstimate(flops=flops, bytes_accessed=0, transcendentals=0),
        name="right",
    )(table, amp, *bufs)


def left_kernel(dims, sizes, table, energy, amp, *refs):
    _, _, row_tiles, shifts, tile = dims
    own, cross, refs = refs[:sizes], refs[sizes : 2 * sizes], refs[2 * sizes :]
    near_own, far_own, near_cross, out, far_cross, left, row_den, held, sems = refs
    half = shifts // 2
    n_q = own[0].shape[1]
    bounds = [0]
    for buf in own:
        bounds.append(bounds[-1] + buf.shape[0])
    for i in range(row_tiles):
        line = energy[2 * shifts + i : 2 * shifts + i + 1, :]
        row_den[i] = jnp.broadcast_to(line, (tile, tile)).T
        source = table[2 * shifts + i]
        shift, other = source % shifts, source // shifts
        rank = jnp.where(shift < half, 0, shifts) + other * half + shift % half
        for n in range(sizes):

            @pl.when((rank >= bounds[n]) & (rank < bounds[n + 1]))
            def _():
                for q in range(n_q):
                    left[i, :, q * tile : (q + 1) * tile] = own[n][rank - bounds[n], q]
                    at = (n_q + q) * tile
                    left[i, :, at : at + tile] = cross[n][rank - bounds[n], q]

    far = [buf for n, buf in enumerate(cross) if bounds[n] >= shifts]
    writes = []
    for part, pieces in enumerate(((near_own, near_cross), (far_own, far_cross))):
        if part:
            right_product(half, dims, table, amp, far, far_cross)
        for m in range(0, shifts, 2):
            cols = slice(m * tile, (m + 2) * tile)
            ids = [part * half + n % half + n // half * shifts for n in (m, m + 1)]
            for i in range(row_tiles):
                rhs = jnp.concatenate(
                    [x[i, q, :, cols] for x in pieces for q in range(n_q)], axis=0
                )
                acc = jnp.dot(left[i], rhs, preferred_element_type=jnp.float32)
                for j, n in enumerate(ids):
                    den = row_den[i] + energy[n : n + 1, :]
                    held[n, i * tile : (i + 1) * tile, :] = (
                        acc[:, j * tile : (j + 1) * tile] / den
                    )
            for n in ids:
                at = pl.ds(pl.multiple_of(table[n] * tile, tile), tile)
                copy = pltpu.make_async_copy(held.at[n], out.at[:, at], sems.at[n])
                copy.start()
                writes.append(copy)
    for copy in writes:
        copy.wait()


def left_product(dims, table, energy, amp, own, cross, done):
    _, _, row_tiles, shifts, tile = dims
    rows, columns = amp.shape
    count, n_q = 2 * shifts, own[0].shape[1]
    return pl.pallas_call(
        functools.partial(left_kernel, dims, len(own)),
        out_shape=jax.ShapeDtypeStruct((rows, columns), jnp.float32),
        in_specs=[SMEM] + [VMEM] * (2 + 2 * len(own) + len(done)),
        out_specs=ANY,
        scratch_shapes=[
            pltpu.VMEM(product_shape(dims, own), jnp.bfloat16),
            pltpu.VMEM((row_tiles, tile, 2 * n_q * tile), jnp.bfloat16),
            pltpu.VMEM((row_tiles, tile, tile), jnp.float32),
            pltpu.VMEM((count, rows, tile), jnp.float32),
            pltpu.SemaphoreType.DMA((count,)),
        ],
        compiler_params=pltpu.CompilerParams(vmem_limit_bytes=24 * 2**20),
        name="left",
    )(table, energy, amp, *own, *cross, *done)


def direct(
    amplitudes, factors, screening, tile_slot, pair_orbitals, occupied_energy, virtual_energy
):
    tile_dev, _, tile, _ = factors.shape
    n_pair, n_cut = lax.axis_size("pair"), lax.axis_size("cuts")
    group = n_pair // screening.shape[0]
    shifts = n_pair // group
    half = shifts // 2
    row_tiles = amplitudes.shape[0] // tile // n_cut

    def send(x, move):
        pairs = [
            (p * n_cut + c, dst[0] * n_cut + dst[1])
            for p in range(n_pair)
            for c in range(n_cut)
            for dst in [move(p, c)]
        ]
        return lax.ppermute(x, BOTH, pairs)

    def over(x):
        return send(x, lambda p, c: (p ^ 1, c))

    dims = (tile_dev, group, row_tiles, shifts, tile)
    given = (screening, tile_slot, factors, pair_orbitals.T, occupied_energy, virtual_energy)
    *picked, table, energy = pick(dims, *given)
    got = [picked[0]] + [
        send(picked[s], lambda p, c: (p ^ (s * group), c))
        for s in range(1, shifts)
    ]
    crossed = [send(got[s], lambda p, c: (p, c ^ 1)) for s in range(shifts)]
    rows = row_tiles * tile
    amp = lax.dynamic_slice_in_dim(amplitudes, lax.axis_index("cuts") * rows, rows, 0)
    quarter = half + half // 2
    sides, done = [], []
    for n, held in enumerate((got, crossed)):
        mine, other = [], []
        for lo, hi in ((0, half), (half, quarter), (quarter, shifts)):
            mine.append(jnp.stack(held[lo:hi]))
            other.append(over(mine[-1]))
        near, far = [mine[0], other[0]], mine[1:] + other[1:]
        sides.append(near + far)
        for m, (base, bufs) in enumerate(((0, near), (half, far))):
            if (n, m) != (1, 1):
                done.append(right(base, dims, table, amp, bufs))
    return left_product(dims, table, energy, amp, *sides, done)


def general(
    amplitudes, factors, screening, tile_slot, pair_orbitals, occupied_energy, virtual_energy
):
    tile_dev, q_cut, tile, _ = factors.shape
    count = screening.shape[1]
    me = lax.axis_index("pair")
    row_tiles = amplitudes.shape[0] // tile
    first_tile = me * row_tiles
    pair_id, tile_start = first_tile // count, first_tile % count
    my_tiles = screening[pair_id]
    my_slots = tile_slot[my_tiles]
    device_pairs = jnp.arange(lax.axis_size("pair"), dtype=jnp.int32) * row_tiles // count
    slot_table = tile_slot[screening[device_pairs]]
    wanted = slot_table // tile_dev == me
    local = jnp.sum(jnp.where(wanted, slot_table % tile_dev, 0), axis=1)
    needed = jnp.any(wanted, axis=1)
    outgoing = jnp.where(
        needed[:, None, None, None], factors[local], jnp.zeros((), factors.dtype)
    )
    incoming = lax.all_to_all(outgoing, "pair", split_axis=0, concat_axis=0, tiled=True)
    chosen = incoming[my_slots // tile_dev]
    left = lax.dynamic_slice_in_dim(chosen, tile_start, row_tiles, 0)
    blocks = amplitudes.reshape(row_tiles, tile, count * tile)
    total = jnp.zeros((row_tiles, tile, count, tile), jnp.float32)
    for q in range(q_cut):
        half = jnp.einsum(
            "iac,icx->iax", left[:, q], blocks, preferred_element_type=jnp.float32
        )
        half = half.astype(jnp.bfloat16).reshape(row_tiles, tile, count, tile)
        total = total + jnp.einsum(
            "iajd,jbd->iajb", half, chosen[:, q], preferred_element_type=jnp.float32
        )
    partial = total.reshape(row_tiles * tile, count * tile).astype(jnp.bfloat16)
    summed = lax.psum_scatter(partial, "cuts", scatter_dimension=0, tiled=True)
    occ = occupied_energy[pair_orbitals[pair_id]]
    energy = virtual_energy[my_tiles].reshape(count * tile)
    rows = summed.shape[0]
    begin = tile_start * tile + lax.axis_index("cuts") * rows
    row_energy = lax.dynamic_slice_in_dim(energy - occ[0], begin, rows, 0)
    return summed.astype(jnp.float32) / (row_energy[:, None] + (energy - occ[1])[None, :])


def solution(mesh):
    n_pair, n_cut = mesh.shape["pair"], mesh.shape["cuts"]

    def build(body):
        return jax.shard_map(
            body,
            mesh=mesh,
            in_specs=(P("pair", None), P("pair", "cuts", None, None), P(), P(), P(), P(), P()),
            out_specs=P(BOTH, None),
            check_vma=False,
        )

    def whole(amplitudes, factors, screening, *rest):
        n_pos, count = screening.shape
        every_owner = count == n_pair and n_pair == 2 * n_pos and n_pos & (n_pos - 1) == 0
        if not (every_owner and n_cut == 2):
            return build(general)(amplitudes, factors, screening, *rest)
        step = build(direct)
        return step(amplitudes, factors, screening, *rest)

    return whole
```
